256 devices in a mesh: tile: 32 (over x, z), owner: 8 (over y, core).
Axes of the slice: x: 4, y: 4, z: 8, core: 2. Of those that a mesh axis runs over, the one named last changes fastest.
Arguments:
- potential: bfloat16 [2, 32, 1024, 256], P(None, 'tile', 'owner'), may hold values from -6 to 6
- positions: int32 [1024, 2], P(('tile', 'owner')), may hold values from 0 to 3840, as said below
- illumination: float32 [2, 256, 256], replicated, may hold values from -5 to 5
- measured: float32 [1024, 256, 256], P(('tile', 'owner')), may hold values from 0 to 2
Outputs:
- gradient: float32 [2, 32, 1024, 256], P(None, 'tile', 'owner')
The draws below stay inside these ranges and needn't reach their ends.
Inputs may be any that keep to these rules, and one draw needn't show every extreme that they name: `positions`: probe p belongs to tile p // 32: its window starts inside that tile and lies inside the object grid, reaching at most into the tiles to the right, below and below-right.
All inputs are finite; a program needn't handle non-finite values.
Results may differ from the reference program's by a relative error of at most 0.0003.
Values may be sent and summed in bfloat16 or wider, within the bound.
No kernel may reach another device: no remote copies, remote signals or barrier semaphores. Data moves between devices by JAX's collectives and lax.ppermute only.
A program may use at most 64 MiB of HBM per device.

```python
import math
import jax
import jax.numpy as jnp
from jax import lax

SLICES = 2
PW = 256
TH = 1024
TW = 256
TX = 8
TILES = 32
GROUP = 32
PROBES = 1024


def draw_positions(key, part):
    indices = jnp.arange(PROBES, dtype=jnp.int32)
    tile_id = indices // GROUP
    tile_row = tile_id // TX
    tile_col = tile_id % TX
    row_limit = jnp.where(tile_row == TILES // TX - 1, TH - PW + 1, TH)
    col_limit = jnp.where(tile_col == TX - 1, TW - PW + 1, TW)
    row_key, col_key = jax.random.split(jax.random.fold_in(key, 11))
    row_draw = jax.random.randint(row_key, (PROBES,), 0, 1 << 30, dtype=jnp.int32) % row_limit
    col_draw = jax.random.randint(col_key, (PROBES,), 0, 1 << 30, dtype=jnp.int32) % col_limit
    member = indices % GROUP
    row_offset = jnp.where(member == 0, row_limit - 1, jnp.where(member == 1, 0, row_draw))
    col_offset = jnp.where(member == 0, col_limit - 1, jnp.where(member == 1, 0, col_draw))
    return jnp.stack([tile_row * TH + row_offset, tile_col * TW + col_offset], axis=1).astype(jnp.int32)


def shard_levels(stream_key, shape, cuts, least, top_value):
    level, own = 1.0, jax.random.fold_in(stream_key, 6)
    for dim, parts in cuts:
        steps = jnp.exp(jax.random.uniform(jax.random.fold_in(own, dim), (parts,), jnp.float32, least / len(cuts), top_value / len(cuts)))
        level = level * jnp.repeat(steps, shape[dim] // parts).reshape([-1 if axis == dim else 1 for axis in range(len(shape))])
    return level


def normal_values(rng, shape, width, limit, shards=(), kind=jnp.bfloat16):
    values = jax.random.normal(rng, shape, jnp.float32) * width
    if len(shards) > 0:
        values = shard_levels(rng, shape, shards, -0.22, 0.18) * values
    return jnp.clip(values, min=-limit, max=limit).astype(kind)


def setup_inputs(seed: int = 0) -> dict:
    keys = jax.random.split(jax.random.key(seed), 5)
    potential = normal_values(keys[0], (SLICES, TILES, TH, TW), 1.0, 6.0, ((1, 32), (2, 8)))
    positions = draw_positions(jax.random.fold_in(keys[4], 71), 0)
    illumination = normal_values(keys[2], (2, PW, PW), 0.7, 5.0, (), jnp.float32)
    measured = jnp.clip(2.0 * jax.random.uniform(keys[3], (PROBES, PW, PW), jnp.float32) ** shard_levels(keys[3], (PROBES, PW, PW), ((0, 256),), -0.2, 0.2), 0.0, 2.0)
    return {"potential": potential, "positions": positions, "illumination": illumination, "measured": measured}


SIGMA = 0.5
LOSS_WEIGHT = 0.125

def probe_loss(window_cut, illumination, measured):
    probe_width = illumination.shape[1]
    counter = jnp.arange(probe_width, dtype=jnp.int32)
    signed = (counter + probe_width // 2) % probe_width - probe_width // 2
    square = (signed * signed).astype(jnp.float32)
    phase_angle = 4.0 * math.pi / (probe_width * probe_width) * (square[:, None] + square[None, :])
    transfer = lax.complex(jnp.cos(phase_angle), -jnp.sin(phase_angle))
    wave = lax.complex(illumination[0], illumination[1])
    layers = window_cut.shape[0]
    for layer_index in range(layers):
        turn = SIGMA * window_cut[layer_index]
        wave = wave * lax.complex(jnp.cos(turn), jnp.sin(turn))
        if layer_index + 1 < layers:
            wave = jnp.fft.ifft2(jnp.fft.fft2(wave, norm='ortho') * transfer, norm='ortho')
    far_field = jnp.fft.fft2(wave, norm='ortho')
    far_real = jnp.real(far_field)
    far_imag = jnp.imag(far_field)
    misfit = far_real * far_real + far_imag * far_imag - measured
    return LOSS_WEIGHT * jnp.sum(misfit * misfit)

def reference(potential, positions, illumination, measured):
    tile_count = TILES // TX
    object_grid = potential.astype(jnp.float32).reshape(SLICES, tile_count, TX, TH, TW)
    object_grid = object_grid.transpose(0, 1, 3, 2, 4).reshape(SLICES, tile_count * TH, TX * TW)
    grad_fn = jax.grad(probe_loss)
    anchor = jnp.zeros((), jnp.int32)

    def probe_step(running, probe_item):
        position, target = probe_item
        corner = (anchor, position[0].astype(jnp.int32), position[1].astype(jnp.int32))
        window_cut = lax.dynamic_slice(object_grid, corner, (SLICES, PW, PW))
        local_grad = grad_fn(window_cut, illumination, target)
        current = lax.dynamic_slice(running, corner, (SLICES, PW, PW))
        return (lax.dynamic_update_slice(running, current + local_grad, corner), None)
    start = jnp.zeros(object_grid.shape, jnp.float32)
    running, _ = lax.scan(probe_step, start, (positions, measured))
    running = running.reshape(SLICES, tile_count, TH, TX, TW).transpose(0, 1, 3, 2, 4)
    return running.reshape(SLICES, TILES, TH, TW)
```

```python
import numpy as np

import jax
import jax.numpy as jnp
from jax import lax
from jax.experimental import pallas as pl
from jax.experimental.pallas import tpu as pltpu
from jax.sharding import PartitionSpec as P

TX = 8
N = 256
H = 128
CH = 16
BF = jnp.bfloat16
F32 = jnp.float32


def real_block(c):
    return np.block([[c.real, -c.imag], [c.imag, c.real]])


def tables():
    k = np.arange(N)
    signed = (k + H) % N - H
    along = np.exp(-4j * np.pi * signed.astype(np.float64) ** 2 / N**2)
    circulant = np.fft.ifft(along)[(k[:, None] - k[None, :]) % N]
    a, b = circulant[:H, :H], circulant[:H, H:]
    m = np.arange(H)
    even = np.exp(-2j * np.pi * ((2 * m[:, None]) * m[None, :] % N) / N) / 16
    odd = np.exp(-2j * np.pi * ((2 * m[:, None] + 1) * m[None, :] % N) / N) / 16
    full = np.stack([real_block(c) for c in ((a + b) / 2, (a - b) / 2, even, odd)])
    high = full.astype(np.float32).astype(jnp.bfloat16)
    low = (full - high.astype(np.float64)).astype(np.float32).astype(jnp.bfloat16)
    return np.stack([high, low], axis=1)


def unshuffle():
    table = np.zeros((N, N), np.float32)
    for q in range(2):
        for n in range(H):
            table[2 * n + q, q * H + n] = 1
    return table.astype(jnp.bfloat16)


def fitted():
    z = (np.cos(np.pi * (np.arange(400) + 0.5) / 400) + 1) * 18.2
    w = np.sqrt(z)
    out = []
    for values, degree in ((np.cos(w / 2), 7), (np.sin(w / 2) / w, 6)):
        fit = np.polynomial.Chebyshev.fit(z, values, degree, domain=[0, 36.4])
        out.append([float(c) for c in fit.convert(kind=np.polynomial.Polynomial).coef])
    return out


COS, SIN = fitted()


def poly(coefficients, z):
    total = jnp.full_like(z, coefficients[-1])
    for c in coefficients[-2::-1]:
        total = total * z + c
    return total


def cossin(w):
    z = w * w
    return poly(COS, z), w * poly(SIN, z)


def split(x):
    high = x.astype(BF)
    return high, (x - high.astype(F32)).astype(BF)


def butterfly(x00, x01, x10, x11):
    a0, a1 = x00 + x10, x01 + x11
    b0, b1 = x00 - x10, x01 - x11
    return a0 + a1, a0 - a1, b0 + b1, b0 - b1


QUADS = [(h, v) for h in range(2) for v in range(2)]


def probes_kernel(pieces, rows, *refs):
    parts, refs = refs[: len(pieces)], refs[len(pieces) :]
    illum, meas, tab, tabt, perm, keep_out, send_out = refs[:7]
    E, O, W, A, B, Z, PS, PH, CS, MP, MS = refs[7:]
    probe_count = meas.shape[0]
    lane = lax.broadcasted_iota(jnp.int32, (CH, H), 1)

    for (place, first_slice, first_col), part in zip(pieces, parts):
        base = pl.multiple_of(rows[place], H)
        slices, height, width = part.shape

        def unpack(i, _, part=part, base=base, slices=slices, width=width, fs=first_slice, fc=first_col):
            r = pl.multiple_of(i * 32, 32)
            for s in range(slices):
                for v in range(width // H):
                    E[fs + s, fc // H + v, pl.ds(base + r, 32), :] = part[
                        s, pl.ds(r, 32), v * H : (v + 1) * H
                    ].astype(F32)
            return 0

        lax.fori_loop(0, height // 32, unpack, 0)

    def clear(i, _):
        r = pl.multiple_of(i * 32, 32)
        for s in range(2):
            for v in range(4):
                O[s, v, pl.ds(r, 32), :] = jnp.zeros((32, H), F32)
        return 0

    lax.fori_loop(0, O.shape[2] // 32, clear, 0)

    def put(r, re, im):
        for pq in range(4):
            p, q = pq // 2, pq % 2
            for j, x in ((0, re[pq]), (1, im[pq])):
                high, low = split(x)
                A[q, pl.ds(p * H + r, CH), j * H : (j + 1) * H] = high
                A[q, pl.ds(p * H + r, CH), N + j * H : N + (j + 1) * H] = low

    def two_sided(t, adjoint):
        left, right = (tabt, tab) if adjoint else (tab, tabt)
        for q in range(2):
            high, low = right[t + q, 0], right[t + q, 1]
            a = A[q]
            v = jnp.dot(
                jnp.concatenate([a, a[:, :N]], axis=1),
                jnp.concatenate([high, high, low], axis=0),
                preferred_element_type=F32,
            )
            for p in range(2):
                for j in range(2):
                    x, y = split(v[p * H : (p + 1) * H, j * H : (j + 1) * H])
                    B[p, 0, j * H : (j + 1) * H, q * H : (q + 1) * H] = x
                    B[p, 1, j * H : (j + 1) * H, q * H : (q + 1) * H] = y
        for p in range(2):
            high, low = left[t + p, 0], left[t + p, 1]
            Z[p] = jnp.dot(
                jnp.concatenate([high, high, low], axis=1),
                jnp.concatenate([B[p, 0], B[p, 1], B[p, 0]], axis=0),
                preferred_element_type=F32,
            )

    def product(r):
        re = [Z[p, pl.ds(r, CH), q * H : (q + 1) * H] for p, q in QUADS]
        im = [Z[p, pl.ds(H + r, CH), q * H : (q + 1) * H] for p, q in QUADS]
        return re, im

    def place(r, h, v):
        return slice(h * H + r, h * H + r + CH), slice(v * H, (v + 1) * H)

    def quads(ref, first, r):
        return [ref[(first, *place(r, h, v))] for h, v in QUADS]

    def probe(n, _):
        r0, c0 = rows[16 + n], rows[24 + n]
        cq, cr = c0 // H, c0 % H
        back = (H - cr) % H
        for s in range(2):
            for k in range(0, N, CH):
                y = [pltpu.roll(E[s, cq + v, pl.ds(r0 + k, CH), :], back, 1) for v in range(3)]
                for v in range(2):
                    W[s, k : k + CH, v * H : (v + 1) * H] = jnp.where(lane < H - cr, y[v], y[v + 1])
        for v in range(2):
            MS[v] = meas[n, :, v * H : (v + 1) * H]
        for p in range(2):
            m = jnp.concatenate([MS[v, pl.ds(p, H, stride=2), :] for v in range(2)], axis=1)
            MP[p] = jnp.dot(
                jnp.concatenate(split(m), axis=1),
                jnp.concatenate([perm[...], perm[...]], axis=0),
                preferred_element_type=F32,
            )
        for r in range(0, H, CH):
            w, a, b = quads(W, 0, r), quads(illum, 0, r), quads(illum, 1, r)
            re, im = [], []
            for i, (h, v) in enumerate(QUADS):
                c, s = cossin(w[i])
                re.append(a[i] * c - b[i] * s)
                im.append(a[i] * s + b[i] * c)
                PS[(0, *place(r, h, v))] = re[i]
                PS[(1, *place(r, h, v))] = im[i]
            put(r, butterfly(*re), butterfly(*im))
        two_sided(0, False)
        for r in range(0, H, CH):
            re, im = product(r)
            re, im = butterfly(*re), butterfly(*im)
            w = quads(W, 1, r)
            xs, ys = [], []
            for i, (h, v) in enumerate(QUADS):
                c, s = cossin(w[i])
                xs.append(re[i] * c - im[i] * s)
                ys.append(re[i] * s + im[i] * c)
                CS[(0, *place(r, h, v))] = c
                CS[(1, *place(r, h, v))] = s
                PH[(0, *place(r, h, v))] = xs[i]
                PH[(1, *place(r, h, v))] = ys[i]
            put(r, butterfly(*xs), butterfly(*ys))
        two_sided(2, False)
        for r in range(0, H, CH):
            re, im = product(r)
            xs, ys = [], []
            for i, (p, q) in enumerate(QUADS):
                m = MP[p, pl.ds(r, CH), q * H : (q + 1) * H]
                misfit = 0.5 * (re[i] * re[i] + im[i] * im[i] - m)
                xs.append(misfit * re[i])
                ys.append(misfit * im[i])
            put(r, xs, ys)
        two_sided(2, True)
        for r in range(0, H, CH):
            re, im = product(r)
            re, im = butterfly(*re), butterfly(*im)
            x, y = quads(PH, 0, r), quads(PH, 1, r)
            c, s = quads(CS, 0, r), quads(CS, 1, r)
            xs, ys = [], []
            for i, (h, v) in enumerate(QUADS):
                W[(1, *place(r, h, v))] = 0.5 * (im[i] * x[i] - re[i] * y[i])
                xs.append(re[i] * c[i] + im[i] * s[i])
                ys.append(im[i] * c[i] - re[i] * s[i])
            put(r, butterfly(*xs), butterfly(*ys))
        two_sided(0, True)
        for r in range(0, H, CH):
            re, im = product(r)
            re, im = butterfly(*re), butterfly(*im)
            x, y = quads(PS, 0, r), quads(PS, 1, r)
            for i, (h, v) in enumerate(QUADS):
                W[(0, *place(r, h, v))] = 0.5 * (im[i] * x[i] - re[i] * y[i])
        for s in range(2):
            for k in range(0, N, CH):
                g = [pltpu.roll(W[s, k : k + CH, v * H : (v + 1) * H], cr, 1) for v in range(2)]
                zero = jnp.zeros_like(g[0])
                here = lane >= cr
                three = jnp.where(here, g[0], zero), jnp.where(here, g[1], g[0]), jnp.where(here, zero, g[1])
                for v, x in enumerate(three):
                    at = (s, cq + v, pl.ds(r0 + k, CH), slice(None))
                    O[at] = O[at] + x
        return 0

    lax.fori_loop(0, probe_count, probe, 0)

    for out, first in ((keep_out, 0), (send_out, 5)):
        for j in range(5):
            base = pl.multiple_of(rows[first + j], H)
            for s in range(2):
                for v in range(4):
                    out[j, s, v] = O[s, v, pl.ds(base, H), :]


def ring(step):
    return [(i, (i + step) % 8) for i in range(8)]


def up(x):
    return lax.ppermute(x, "owner", ring(2))


def down(x):
    return lax.ppermute(x, "owner", ring(-2))


def twin(x):
    return lax.ppermute(x, "owner", [(i, i ^ 1) for i in range(8)])


def shift_cols(x, step):
    tiles = lax.axis_size("tile")
    return lax.ppermute(x, "tile", [(i, i + step) for i in range(tiles) if 0 <= i % TX + step < TX])


def shift_rows(x, step):
    tiles = lax.axis_size("tile")
    return lax.ppermute(x, "tile", [(i, i + step * TX) for i in range(tiles) if 0 <= i + step * TX < tiles])


def body(potential, positions, illumination, measured):
    own = potential[:, 0]
    layers, height, width = own.shape
    tile = lax.axis_index("tile")
    owner = lax.axis_index("owner")
    y, core = owner // 2, owner % 2
    own_up, own_down = up(own), down(own)
    right = shift_cols(own, -1)
    right_up, right_down = up(right), down(right)
    own_far = up(own_up[:1]), down(own_down[1:])
    right_far = up(right_up[:1]), down(right_down[1:])
    mine = [(0, 0, 0, own), (1, 0, 0, own_up), (2, 0, 0, own_down)]
    mine += [(0, 0, N, right), (1, 0, N, right_up), (2, 0, N, right_down)]
    mine += [(3, 0, 0, own_far[0]), (3, 1, 0, own_far[1])]
    mine += [(3, 0, N, right_far[0]), (3, 1, N, right_far[1])]
    opposite = jnp.concatenate([jnp.concatenate(own_far), jnp.concatenate(right_far)], axis=2)
    first = lax.select_n(
        y,
        jnp.concatenate([own, right], axis=2),
        jnp.concatenate([own_up, right_up], axis=2),
        opposite,
        jnp.concatenate([own_down, right_down], axis=2),
    )
    mine.append((4, 0, 0, shift_rows(first, -1)))
    pieces = mine + [(k + 5, s, c, twin(x)) for k, s, c, x in mine]

    chips = jnp.stack([y, (y + 3) % 4, (y + 1) % 4, (y + 2) % 4, jnp.full_like(y, 4)])
    bases = jnp.concatenate([(2 * chips + core) * H, (2 * chips + 1 - core) * H])
    row_start = positions[:, 0] - tile // TX * (8 * height)
    col_start = positions[:, 1] - tile % TX * width
    fill = jnp.zeros((4,), jnp.int32)
    rows = jnp.concatenate([bases, jnp.zeros((6,), jnp.int32), row_start, fill, col_start, fill])

    table = tables()
    smem = pl.BlockSpec(memory_space=pltpu.SMEM)
    vmem = pl.BlockSpec(memory_space=pltpu.VMEM)
    field = pltpu.VMEM((2, N, N), F32)
    extended = pltpu.VMEM((layers, 4, 10 * H, H), F32)
    part = jax.ShapeDtypeStruct((5, layers, 4, H, H), F32)
    operands = [x for *_, x in pieces]
    operands += [illumination, measured]
    operands += [jnp.asarray(table), jnp.asarray(np.ascontiguousarray(np.swapaxes(table, 2, 3)))]
    operands += [jnp.asarray(unshuffle())]

    def kernel(*refs):
        probes_kernel([(k, s, c) for k, s, c, _ in pieces], *refs)

    keep, send = pl.pallas_call(
        kernel,
        out_shape=(part, part),
        in_specs=[smem] + [vmem] * len(operands),
        out_specs=(vmem, vmem),
        scratch_shapes=[
            extended,
            extended,
            field,
            pltpu.VMEM((2, N, 2 * N), BF),
            pltpu.VMEM((2, 2, N, N), BF),
            field,
            field,
            field,
            field,
            pltpu.VMEM((2, H, N), F32),
            pltpu.VMEM((2, N, H), F32),
        ],
        compiler_params=pltpu.CompilerParams(vmem_limit_bytes=40 << 20),
        name="probes",
    )(rows, *operands)

    total = keep + twin(send)
    below = shift_rows(total[4], 1)
    here = [total[j] + jnp.where((y + d) % 4 == 0, below, 0) for j, d in enumerate((0, 3, 1, 2))]
    opposite = here[3]
    relay_up, relay_down = up(opposite[:1]), down(opposite[1:])
    zero = jnp.zeros_like(relay_up)
    after = here[2] + jnp.concatenate([relay_up, zero])
    before = here[1] + jnp.concatenate([zero, relay_down])
    result = here[0] + up(after) + down(before)
    result = result[:, :2] + shift_cols(result[:, 2:], 1)
    result = jnp.concatenate([result[:, 0], result[:, 1]], axis=2)
    return result[:, None]


def solution(mesh):
    in_specs = (
        P(None, "tile", "owner", None),
        P(("tile", "owner"), None),
        P(),
        P(("tile", "owner"), None, None),
    )
    out_specs = P(None, "tile", "owner", None)
    return jax.shard_map(body, mesh=mesh, in_specs=in_specs, out_specs=out_specs, check_vma=False)
```

```python
import numpy as np

import jax
import jax.numpy as jnp
from jax import lax
from jax.experimental import pallas as pl
from jax.experimental.pallas import tpu as pltpu
from jax.sharding import PartitionSpec as P

TX = 8
N = 256
H = 128
CH = 16
BF = jnp.bfloat16
F32 = jnp.float32


def real_block(c):
    return np.block([[c.real, -c.imag], [c.imag, c.real]])


def tables():
    k = np.arange(N)
    signed = (k + H) % N - H
    along = np.exp(-4j * np.pi * signed.astype(np.float64) ** 2 / N**2)
    circulant = np.fft.ifft(along)[(k[:, None] - k[None, :]) % N]
    a, b = circulant[:H, :H], circulant[:H, H:]
    m = np.arange(H)
    even = np.exp(-2j * np.pi * ((2 * m[:, None]) * m[None, :] % N) / N) / 16
    odd = np.exp(-2j * np.pi * ((2 * m[:, None] + 1) * m[None, :] % N) / N) / 16
    full = np.stack([real_block(c) for c in ((a + b) / 2, (a - b) / 2, even, odd)])
    high = full.astype(np.float32).astype(jnp.bfloat16)
    low = (full - high.astype(np.float64)).astype(np.float32).astype(jnp.bfloat16)
    return np.stack([high, low], axis=1)


def unshuffle():
    table = np.zeros((N, N), np.float32)
    for q in range(2):
        for n in range(H):
            table[2 * n + q, q * H + n] = 1
    return table.astype(jnp.bfloat16)


def fitted():
    z = (np.cos(np.pi * (np.arange(400) + 0.5) / 400) + 1) * 18.2
    w = np.sqrt(z)
    out = []
    for values, degree in ((np.cos(w / 2), 7), (np.sin(w / 2) / w, 6)):
        fit = np.polynomial.Chebyshev.fit(z, values, degree, domain=[0, 36.4])
        out.append([float(c) for c in fit.convert(kind=np.polynomial.Polynomial).coef])
    return out


COS, SIN = fitted()


def poly(coefficients, z):
    total = jnp.full_like(z, coefficients[-1])
    for c in coefficients[-2::-1]:
        total = total * z + c
    return total


def cossin(w):
    z = w * w
    return poly(COS, z), w * poly(SIN, z)


def split(x):
    high = x.astype(BF)
    return high, (x - high.astype(F32)).astype(BF)


def butterfly(x00, x01, x10, x11):
    a0, a1 = x00 + x10, x01 + x11
    b0, b1 = x00 - x10, x01 - x11
    return a0 + a1, a0 - a1, b0 + b1, b0 - b1


QUADS = [(h, v) for h in range(2) for v in range(2)]


def probes_kernel(pieces, *refs):
    count = len(pieces)
    sources, parts, refs = refs[:7], list(refs[7 : 6 + count]), refs[6 + count :]
    keep_out, send_out = refs[:2]
    E, O, W, A, B, Z, PS, PH, CS, MP, MS = refs[2:13]
    positions, here, illum, meas, tab, tabt, perm, sems = refs[13:]
    copies = [
        pltpu.make_async_copy(source, target, sems.at[i])
        for i, (source, target) in enumerate(zip(sources, (positions, here, illum, meas, tab, tabt, perm)))
    ]
    for copy in copies:
        copy.start()
    tile = lax.axis_index("tile")
    owner = lax.axis_index("owner")
    chip, core = owner // 2, owner % 2

    def first_row(step, other):
        chip_rows = 8 if step is None else 2 * ((chip + step) % 4)
        return pl.multiple_of((chip_rows + (1 - core if other else core)) * H, H)

    probe_count = meas.shape[0]
    lane = lax.broadcasted_iota(jnp.int32, (CH, H), 1)

    def clear(i, _):
        r = pl.multiple_of(i * 32, 32)
        for s in range(2):
            for v in range(4):
                O[s, v, pl.ds(r, 32), :] = jnp.zeros((32, H), F32)
        return 0

    lax.fori_loop(0, O.shape[2] // 32, clear, 0)
    copies[1].wait()
    parts.insert(0, here)
    for (step, other, first_slice, first_col), part in zip(pieces, parts):
        base = first_row(step, other)
        slices, height, width = part.shape

        def unpack(i, _, part=part, base=base, slices=slices, width=width, fs=first_slice, fc=first_col):
            r = pl.multiple_of(i * 32, 32)
            for s in range(slices):
                for v in range(width // H):
                    E[fs + s, fc // H + v, pl.ds(base + r, 32), :] = part[
                        s, pl.ds(r, 32), v * H : (v + 1) * H
                    ].astype(F32)
            return 0

        lax.fori_loop(0, height // 32, unpack, 0)
    for i in (0, 2, 3, 4, 5, 6):
        copies[i].wait()
    def put(r, re, im):
        for pq in range(4):
            p, q = pq // 2, pq % 2
            for j, x in ((0, re[pq]), (1, im[pq])):
                high, low = split(x)
                A[q, pl.ds(p * H + r, CH), j * H : (j + 1) * H] = high
                A[q, pl.ds(p * H + r, CH), N + j * H : N + (j + 1) * H] = low

    def two_sided(t, adjoint):
        left, right = (tabt, tab) if adjoint else (tab, tabt)
        for q in range(2):
            high, low = right[t + q, 0], right[t + q, 1]
            a = A[q]
            v = jnp.dot(
                jnp.concatenate([a, a[:, :N]], axis=1),
                jnp.concatenate([high, high, low], axis=0),
                preferred_element_type=F32,
            )
            for p in range(2):
                for j in range(2):
                    x, y = split(v[p * H : (p + 1) * H, j * H : (j + 1) * H])
                    B[p, 0, j * H : (j + 1) * H, q * H : (q + 1) * H] = x
                    B[p, 1, j * H : (j + 1) * H, q * H : (q + 1) * H] = y
        for p in range(2):
            high, low = left[t + p, 0], left[t + p, 1]
            Z[p] = jnp.dot(
                jnp.concatenate([high, high, low], axis=1),
                jnp.concatenate([B[p, 0], B[p, 1], B[p, 0]], axis=0),
                preferred_element_type=F32,
            )

    def product(r):
        re = [Z[p, pl.ds(r, CH), q * H : (q + 1) * H] for p, q in QUADS]
        im = [Z[p, pl.ds(H + r, CH), q * H : (q + 1) * H] for p, q in QUADS]
        return re, im

    def place(r, h, v):
        return slice(h * H + r, h * H + r + CH), slice(v * H, (v + 1) * H)

    def quads(ref, first, r):
        return [ref[(first, *place(r, h, v))] for h, v in QUADS]

    def probe(n, _):
        r0 = positions[0, n] - tile // TX * (8 * H)
        c0 = positions[1, n] - tile % TX * N
        cq, cr = c0 // H, c0 % H
        back = (H - cr) % H
        for s in range(2):
            for k in range(0, N, CH):
                y = [pltpu.roll(E[s, cq + v, pl.ds(r0 + k, CH), :], back, 1) for v in range(3)]
                for v in range(2):
                    W[s, k : k + CH, v * H : (v + 1) * H] = jnp.where(lane < H - cr, y[v], y[v + 1])
        for v in range(2):
            MS[v] = meas[n, :, v * H : (v + 1) * H]
        for p in range(2):
            m = jnp.concatenate([MS[v, pl.ds(p, H, stride=2), :] for v in range(2)], axis=1)
            MP[p] = jnp.dot(
                jnp.concatenate(split(m), axis=1),
                jnp.concatenate([perm[...], perm[...]], axis=0),
                preferred_element_type=F32,
            )
        for r in range(0, H, CH):
            w, a, b = quads(W, 0, r), quads(illum, 0, r), quads(illum, 1, r)
            re, im = [], []
            for i, (h, v) in enumerate(QUADS):
                c, s = cossin(w[i])
                re.append(a[i] * c - b[i] * s)
                im.append(a[i] * s + b[i] * c)
                PS[(0, *place(r, h, v))] = re[i]
                PS[(1, *place(r, h, v))] = im[i]
            put(r, butterfly(*re), butterfly(*im))
        two_sided(0, False)
        for r in range(0, H, CH):
            re, im = product(r)
            re, im = butterfly(*re), butterfly(*im)
            w = quads(W, 1, r)
            xs, ys = [], []
            for i, (h, v) in enumerate(QUADS):
                c, s = cossin(w[i])
                xs.append(re[i] * c - im[i] * s)
                ys.append(re[i] * s + im[i] * c)
                CS[(0, *place(r, h, v))] = c
                CS[(1, *place(r, h, v))] = s
                PH[(0, *place(r, h, v))] = xs[i]
                PH[(1, *place(r, h, v))] = ys[i]
            put(r, butterfly(*xs), butterfly(*ys))
        two_sided(2, False)
        for r in range(0, H, CH):
            re, im = product(r)
            xs, ys = [], []
            for i, (p, q) in enumerate(QUADS):
                m = MP[p, pl.ds(r, CH), q * H : (q + 1) * H]
                misfit = 0.5 * (re[i] * re[i] + im[i] * im[i] - m)
                xs.append(misfit * re[i])
                ys.append(misfit * im[i])
            put(r, xs, ys)
        two_sided(2, True)
        for r in range(0, H, CH):
            re, im = product(r)
            re, im = butterfly(*re), butterfly(*im)
            x, y = quads(PH, 0, r), quads(PH, 1, r)
            c, s = quads(CS, 0, r), quads(CS, 1, r)
            xs, ys = [], []
            for i, (h, v) in enumerate(QUADS):
                W[(1, *place(r, h, v))] = 0.5 * (im[i] * x[i] - re[i] * y[i])
                xs.append(re[i] * c[i] + im[i] * s[i])
                ys.append(im[i] * c[i] - re[i] * s[i])
            put(r, butterfly(*xs), butterfly(*ys))
        two_sided(0, True)
        for r in range(0, H, CH):
            re, im = product(r)
            re, im = butterfly(*re), butterfly(*im)
            x, y = quads(PS, 0, r), quads(PS, 1, r)
            for i, (h, v) in enumerate(QUADS):
                W[(0, *place(r, h, v))] = 0.5 * (im[i] * x[i] - re[i] * y[i])
        for s in range(2):
            for k in range(0, N, CH):
                g = [pltpu.roll(W[s, k : k + CH, v * H : (v + 1) * H], cr, 1) for v in range(2)]
                zero = jnp.zeros_like(g[0])
                here = lane >= cr
                three = jnp.where(here, g[0], zero), jnp.where(here, g[1], g[0]), jnp.where(here, zero, g[1])
                for v, x in enumerate(three):
                    at = (s, cq + v, pl.ds(r0 + k, CH), slice(None))
                    O[at] = O[at] + x
        return 0

    lax.fori_loop(0, probe_count, probe, 0)

    for out, other in ((keep_out, False), (send_out, True)):
        for j, step in enumerate(STEPS):
            base = first_row(step, other)
            for s in range(2):
                for v in range(4):
                    out[j, s, v] = O[s, v, pl.ds(base, H), :]


STEPS = (0, 3, 1, 2, None)
LEVELS = 32766.0


def rows_of(blocks):
    return blocks * H + CH


def encode(blocks, out):
    sublane = lax.broadcasted_iota(jnp.int32, (CH, H), 0)
    logs = jnp.zeros((CH, H), F32)
    for b, block in enumerate(blocks):
        top = jnp.abs(block(0))
        for r in range(CH, H, CH):
            top = jnp.maximum(top, jnp.abs(block(r)))
        top = jnp.max(top, axis=0, keepdims=True)
        log = jnp.ceil(16.0 * jnp.log2(jnp.maximum(top, 1e-30)))
        factor = LEVELS * jnp.exp2(log * (-1.0 / 16.0))
        for r in range(0, H, CH):
            out[b * H + r : b * H + r + CH, :] = jnp.round(block(r) * factor).astype(jnp.int32).astype(jnp.int16)
        logs = jnp.where(sublane == b, log, logs)
    n = len(blocks) * H
    out[n : n + CH, :] = logs.astype(jnp.int32).astype(jnp.int16)


def decoder(code, count):
    n = count * H
    logs = code[n : n + CH, :].astype(jnp.int32).astype(F32)
    scales = jnp.exp2(logs * (1.0 / 16.0)) * (1.0 / LEVELS)

    def rows(b, r, factor=None):
        scale = scales[b : b + 1, :]
        if factor is not None:
            scale = scale * factor
        return code[b * H + r : b * H + r + CH, :].astype(jnp.int32).astype(F32) * scale

    return rows


def here_sum(keep, came, below):
    chip = lax.axis_index("owner") // 2
    both, even, odd = below
    gets = decoder(both, 8), (decoder(even, 4), decoder(odd, 4))

    def cells(j, s, v, r):
        x = keep[j, s, v, r : r + CH, :] + came[j, s, v, r : r + CH, :]
        factor = jnp.where((chip + STEPS[j]) % 4 == 0, 1.0, 0.0)
        return x + gets[0](s * 4 + v, r, factor) + gets[1][s](v, r, factor)

    return cells


def block_of(total, s, v):
    return lambda r: total[s, v, r : r + CH, :]


def below_kernel(keep, came, both, even, odd, total):
    for s in range(2):
        for v in range(4):
            total[s, v] = keep[4, s, v] + came[4, s, v]
    encode([block_of(total, s, v) for s in range(2) for v in range(4)], both)
    for s, out in ((0, even), (1, odd)):
        encode([block_of(total, s, v) for v in range(4)], out)


def relay_kernel(keep, came, out_up, out_down, total):
    for s, out in ((0, out_up), (1, out_down)):
        for v in range(4):
            total[s, v] = keep[3, s, v] + came[3, s, v]
        encode([block_of(total, s, v) for v in range(4)], out)


def sides_kernel(keep, came, *refs):
    cells = here_sum(keep, came, refs[:3])
    from_up, from_down, up, down, total = refs[3:]
    for j, slice_, code, out in ((2, 0, from_up, up), (1, 1, from_down, down)):
        get = decoder(code, 4)
        for s in range(2):
            for v in range(4):
                for r in range(0, H, CH):
                    x = cells(j, s, v, r)
                    total[s, v, r : r + CH, :] = x + get(v, r) if s == slice_ else x
        encode([block_of(total, s, v) for s in range(2) for v in range(4)], out)


def own_kernel(keep, came, *refs):
    cells = here_sum(keep, came, refs[:3])
    gets = [decoder(code, 8) for code in refs[3:5]]
    left, over, total = refs[5:]
    for s in range(2):
        for v in range(4):
            for r in range(0, H, CH):
                x = cells(0, s, v, r)
                for get in gets:
                    x = x + get(s * 4 + v, r)
                if v < 2:
                    left[s, v, r : r + CH, :] = x
                else:
                    total[s, v, r : r + CH, :] = x
    encode([block_of(total, s, v) for s in range(2) for v in (2, 3)], over)


def last_kernel(left, code, out):
    get = decoder(code, 4)
    for s in range(2):
        for v in range(2):
            for r in range(0, H, CH):
                out[s, r : r + CH, v * H : (v + 1) * H] = left[s, v, r : r + CH, :] + get(s * 2 + v, r)


def local(kernel, name, outs, *operands, scratch=True):
    vmem = pl.BlockSpec(memory_space=pltpu.VMEM)
    return pl.pallas_call(
        kernel,
        out_shape=tuple(outs),
        in_specs=[vmem] * len(operands),
        out_specs=(vmem,) * len(outs),
        scratch_shapes=[pltpu.VMEM((2, 4, H, H), F32)] if scratch else [],
        compiler_params=pltpu.CompilerParams(vmem_limit_bytes=16 << 20),
        name=name,
    )(*operands)


def twin(x):
    return lax.ppermute(x, "owner", [(i, i ^ 1) for i in range(lax.axis_size("owner"))])


def hop(x, tile_rows=0, tile_cols=0, chips=0, only=range(4)):
    owners, tiles = lax.axis_size("owner"), lax.axis_size("tile")
    route = []
    for t in range(tiles):
        row, col = t // TX + tile_rows, t % TX + tile_cols
        if 0 <= row < tiles // TX and 0 <= col < TX:
            for o in range(owners):
                if o // 2 in only:
                    route.append((t * owners + o, (row * TX + col) * owners + (o + 2 * chips) % owners))
    return lax.ppermute(x, ("tile", "owner"), route)


def body(potential, positions, illumination, measured):
    own = potential[:, 0]
    layers = own.shape[0]
    chip = lax.axis_index("owner") // 2
    own_up, own_down = hop(own, chips=1), hop(own, chips=-1)
    right = hop(own, tile_cols=-1)
    right_up, right_down = hop(right, chips=1), hop(right, chips=-1)
    own_far = hop(own_up[:1], chips=1), hop(own_down[1:], chips=-1)
    right_far = hop(right_up[:1], chips=1), hop(right_down[1:], chips=-1)
    first = jnp.concatenate(
        [lax.select_n(chip, own, own_up, own, own_down), lax.select_n(chip, right, right_up, right, right_down)],
        axis=2,
    )
    low = (
        hop(first[:1], tile_rows=-1, chips=1, only=(1,)),
        hop(first[1:], tile_rows=-1, chips=-1, only=(3,)),
        hop(first, tile_rows=-1, only=(0, 1, 3)),
    )

    near = (own, own_up, own_down, right, right_up, right_down)
    near_twins = [twin(x) for x in near]
    low, own_far, right_far, near_twins = lax.optimization_barrier((low, own_far, right_far, near_twins))
    low = jnp.where(chip == 2, jnp.concatenate(low[:2]), low[2])

    table = tables()
    fixed = [positions.T, own, illumination, measured]
    fixed += [jnp.asarray(table), jnp.asarray(np.ascontiguousarray(np.swapaxes(table, 2, 3)))]
    fixed += [jnp.asarray(unshuffle())]
    fixed = [pltpu.with_memory_space_constraint(x, pltpu.HBM) for x in fixed]
    vmem = pl.BlockSpec(memory_space=pltpu.VMEM)
    hbm = pl.BlockSpec(memory_space=pltpu.HBM)
    mine = [(0, 0, 0, own), (3, 0, 0, own_up), (1, 0, 0, own_down)]
    mine += [(0, 0, N, right), (3, 0, N, right_up), (1, 0, N, right_down)]
    mine += [(2, 0, 0, own_far[0]), (2, 1, 0, own_far[1])]
    mine += [(2, 0, N, right_far[0]), (2, 1, N, right_far[1])]
    mine.append((None, 0, 0, low))
    pieces = [(k, False, s, c) for k, s, c, _ in mine] + [(k, True, s, c) for k, s, c, _ in mine]
    cells = [x for *_, x in mine[1:]] + near_twins + [twin(x) for *_, x in mine[6:]]

    field = pltpu.VMEM((2, N, N), F32)
    extended = pltpu.VMEM((layers, 4, 10 * H, H), F32)
    part = jax.ShapeDtypeStruct((5, layers, 4, H, H), F32)

    def kernel(*refs):
        probes_kernel(pieces, *refs)

    keep, send = pl.pallas_call(
        kernel,
        out_shape=(part, part),
        in_specs=[hbm] * len(fixed) + [vmem] * len(cells),
        out_specs=(vmem, vmem),
        scratch_shapes=[
            extended,
            extended,
            field,
            pltpu.VMEM((2, N, 2 * N), BF),
            pltpu.VMEM((2, 2, N, N), BF),
            field,
            field,
            field,
            field,
            pltpu.VMEM((2, H, N), F32),
            pltpu.VMEM((2, N, H), F32),
            pltpu.SMEM((2, 4), jnp.int32),
            *[pltpu.VMEM(x.shape, x.dtype) for x in fixed[1:]],
            pltpu.SemaphoreType.DMA((7,)),
        ],
        compiler_params=pltpu.CompilerParams(vmem_limit_bytes=36 << 20),
        name="probes",
    )(*fixed, *cells)

    whole = jax.ShapeDtypeStruct((rows_of(8), H), jnp.int16)
    half = jax.ShapeDtypeStruct((rows_of(4), H), jnp.int16)
    came = twin(send)
    both, even, odd = local(below_kernel, "below", [whole, half, half], keep, came)
    below = (
        hop(both, tile_rows=1, only=(0, 1, 3)),
        hop(even, tile_rows=1, chips=-1, only=(2,)),
        hop(odd, tile_rows=1, chips=1, only=(2,)),
    )
    from_up, from_down = local(relay_kernel, "relay", [half, half], keep, came)
    from_up, from_down = hop(from_up, chips=1), hop(from_down, chips=-1)
    to_up, to_down = local(sides_kernel, "sides", [whole] * 2, keep, came, *below, from_up, from_down)
    to_up, to_down = hop(to_up, chips=1), hop(to_down, chips=-1)
    left = jax.ShapeDtypeStruct((layers, 2, H, H), F32)
    left, over = local(own_kernel, "own", [left, half], keep, came, *below, to_up, to_down)
    over = hop(over, tile_cols=1)
    result = jax.ShapeDtypeStruct((layers, H, N), F32)
    (result,) = local(last_kernel, "last", [result], left, over, scratch=False)
    return result[:, None]


def solution(mesh):
    in_specs = (
        P(None, "tile", "owner", None),
        P(("tile", "owner"), None),
        P(),
        P(("tile", "owner"), None, None),
    )
    out_specs = P(None, "tile", "owner", None)
    return jax.shard_map(body, mesh=mesh, in_specs=in_specs, out_specs=out_specs, check_vma=False)
```

```python
import numpy as np

import jax
import jax.numpy as jnp
from jax import lax
from jax.experimental import pallas as pl
from jax.experimental.pallas import tpu as pltpu
from jax.sharding import PartitionSpec as P

TX = 8
N = 256
H = 128
CH = 16
BF = jnp.bfloat16
F32 = jnp.float32


def real_block(c):
    return np.block([[c.real, -c.imag], [c.imag, c.real]])


def tables():
    k = np.arange(N)
    signed = (k + H) % N - H
    along = np.exp(-4j * np.pi * signed.astype(np.float64) ** 2 / N**2)
    circulant = np.fft.ifft(along)[(k[:, None] - k[None, :]) % N]
    a, b = circulant[:H, :H], circulant[:H, H:]
    m = np.arange(H)
    even = np.exp(-2j * np.pi * ((2 * m[:, None]) * m[None, :] % N) / N) / 16
    odd = np.exp(-2j * np.pi * ((2 * m[:, None] + 1) * m[None, :] % N) / N) / 16
    full = np.stack([real_block(c) for c in ((a + b) / 2, (a - b) / 2, even, odd)])
    high = full.astype(np.float32).astype(jnp.bfloat16)
    low = (full - high.astype(np.float64)).astype(np.float32).astype(jnp.bfloat16)
    return np.stack([high, low], axis=1)


def unshuffle():
    table = np.zeros((N, N), np.float32)
    for q in range(2):
        for n in range(H):
            table[2 * n + q, q * H + n] = 1
    return table.astype(jnp.bfloat16)


def fitted():
    z = (np.cos(np.pi * (np.arange(400) + 0.5) / 400) + 1) * 18.2
    w = np.sqrt(z)
    out = []
    for values, degree in ((np.cos(w / 2), 7), (np.sin(w / 2) / w, 6)):
        fit = np.polynomial.Chebyshev.fit(z, values, degree, domain=[0, 36.4])
        out.append([float(c) for c in fit.convert(kind=np.polynomial.Polynomial).coef])
    return out


COS, SIN = fitted()


def poly(coefficients, z):
    total = jnp.full_like(z, coefficients[-1])
    for c in coefficients[-2::-1]:
        total = total * z + c
    return total


def cossin(w):
    z = w * w
    return poly(COS, z), w * poly(SIN, z)


def split(x):
    high = x.astype(BF)
    return high, (x - high.astype(F32)).astype(BF)


def butterfly(x00, x01, x10, x11):
    a0, a1 = x00 + x10, x01 + x11
    b0, b1 = x00 - x10, x01 - x11
    return a0 + a1, a0 - a1, b0 + b1, b0 - b1


QUADS = [(h, v) for h in range(2) for v in range(2)]


def probes_kernel(pieces, *refs):
    count = len(pieces)
    sources, parts, refs = refs[:7], list(refs[7 : 6 + count]), refs[6 + count :]
    keep_out, early_out, late_out = refs[:3]
    E, O, *work = refs[3:14]
    positions, here, illum, meas, tab, tabt, perm, sems = refs[14:]
    copies = [
        pltpu.make_async_copy(source, target, sems.at[i])
        for i, (source, target) in enumerate(zip(sources, (positions, here, illum, meas, tab, tabt, perm)))
    ]
    for copy in copies:
        copy.start()
    tile = lax.axis_index("tile")
    owner = lax.axis_index("owner")
    chip, core = owner // 2, owner % 2

    def first_row(step, other):
        chip_rows = 8 if step is None else 2 * ((chip + step) % 4)
        return pl.multiple_of((chip_rows + (1 - core if other else core)) * H, H)

    probe_count = meas.shape[0]
    lane = lax.broadcasted_iota(jnp.int32, (CH, H), 1)

    def clear(i, _):
        r = pl.multiple_of(i * 32, 32)
        for s in range(2):
            for v in range(4):
                O[s, v, pl.ds(r, 32), :] = jnp.zeros((32, H), F32)
        return 0

    lax.fori_loop(0, O.shape[2] // 32, clear, 0)
    copies[1].wait()
    parts.insert(0, here)
    for (step, other, first_slice, first_col), part in zip(pieces, parts):
        base = first_row(step, other)
        slices, height, width = part.shape

        def unpack(i, _, part=part, base=base, slices=slices, width=width, fs=first_slice, fc=first_col):
            r = pl.multiple_of(i * 32, 32)
            for s in range(slices):
                for v in range(width // H):
                    E[fs + s, fc // H + v, pl.ds(base + r, 32), :] = part[
                        s, pl.ds(r, 32), v * H : (v + 1) * H
                    ].astype(F32)
            return 0

        lax.fori_loop(0, height // 32, unpack, 0)
    for i in (0, 2, 3, 4, 5, 6):
        copies[i].wait()
    def chain(slot):
        W, A, B, Z, PS, PH, CS, MP, MS = (ref.at[slot] for ref in work)

        def put(r, re, im):
            for pq in range(4):
                p, q = pq // 2, pq % 2
                for j, x in ((0, re[pq]), (1, im[pq])):
                    high, low = split(x)
                    A[q, pl.ds(p * H + r, CH), j * H : (j + 1) * H] = high
                    A[q, pl.ds(p * H + r, CH), N + j * H : N + (j + 1) * H] = low

        def two_sided(t, adjoint):
            left, right = (tabt, tab) if adjoint else (tab, tabt)
            for q in range(2):
                high, low = right[t + q, 0], right[t + q, 1]
                a = A[q]
                v = jnp.dot(
                    jnp.concatenate([a, a[:, :N]], axis=1),
                    jnp.concatenate([high, high, low], axis=0),
                    preferred_element_type=F32,
                )
                for p in range(2):
                    for j in range(2):
                        x, y = split(v[p * H : (p + 1) * H, j * H : (j + 1) * H])
                        B[p, 0, j * H : (j + 1) * H, q * H : (q + 1) * H] = x
                        B[p, 1, j * H : (j + 1) * H, q * H : (q + 1) * H] = y
            for p in range(2):
                high, low = left[t + p, 0], left[t + p, 1]
                Z[p] = jnp.dot(
                    jnp.concatenate([high, high, low], axis=1),
                    jnp.concatenate([B[p, 0], B[p, 1], B[p, 0]], axis=0),
                    preferred_element_type=F32,
                )

        def product(r):
            re = [Z[p, pl.ds(r, CH), q * H : (q + 1) * H] for p, q in QUADS]
            im = [Z[p, pl.ds(H + r, CH), q * H : (q + 1) * H] for p, q in QUADS]
            return re, im

        def place(r, h, v):
            return slice(h * H + r, h * H + r + CH), slice(v * H, (v + 1) * H)

        def quads(ref, first, r):
            return [ref[(first, *place(r, h, v))] for h, v in QUADS]

        def probe(n):
            r0 = positions[0, n] - tile // TX * (8 * H)
            c0 = positions[1, n] - tile % TX * N
            cq, cr = c0 // H, c0 % H
            back = (H - cr) % H
            for s in range(2):
                for k in range(0, N, CH):
                    y = [pltpu.roll(E[s, cq + v, pl.ds(r0 + k, CH), :], back, 1) for v in range(3)]
                    for v in range(2):
                        W[s, k : k + CH, v * H : (v + 1) * H] = jnp.where(lane < H - cr, y[v], y[v + 1])
            yield
            for v in range(2):
                MS[v] = meas[n, :, v * H : (v + 1) * H]
            for p in range(2):
                m = jnp.concatenate([MS[v, pl.ds(p, H, stride=2), :] for v in range(2)], axis=1)
                MP[p] = jnp.dot(
                    jnp.concatenate(split(m), axis=1),
                    jnp.concatenate([perm[...], perm[...]], axis=0),
                    preferred_element_type=F32,
                )
            yield
            for r in range(0, H, CH):
                w, a, b = quads(W, 0, r), quads(illum, 0, r), quads(illum, 1, r)
                re, im = [], []
                for i, (h, v) in enumerate(QUADS):
                    c, s = cossin(w[i])
                    re.append(a[i] * c - b[i] * s)
                    im.append(a[i] * s + b[i] * c)
                    PS[(0, *place(r, h, v))] = re[i]
                    PS[(1, *place(r, h, v))] = im[i]
                put(r, butterfly(*re), butterfly(*im))
            yield
            two_sided(0, False)
            yield
            for r in range(0, H, CH):
                re, im = product(r)
                re, im = butterfly(*re), butterfly(*im)
                w = quads(W, 1, r)
                xs, ys = [], []
                for i, (h, v) in enumerate(QUADS):
                    c, s = cossin(w[i])
                    xs.append(re[i] * c - im[i] * s)
                    ys.append(re[i] * s + im[i] * c)
                    CS[(0, *place(r, h, v))] = c
                    CS[(1, *place(r, h, v))] = s
                    PH[(0, *place(r, h, v))] = xs[i]
                    PH[(1, *place(r, h, v))] = ys[i]
                put(r, butterfly(*xs), butterfly(*ys))
            yield
            two_sided(2, False)
            yield
            for r in range(0, H, CH):
                re, im = product(r)
                xs, ys = [], []
                for i, (p, q) in enumerate(QUADS):
                    m = MP[p, pl.ds(r, CH), q * H : (q + 1) * H]
                    misfit = 0.5 * (re[i] * re[i] + im[i] * im[i] - m)
                    xs.append(misfit * re[i])
                    ys.append(misfit * im[i])
                put(r, xs, ys)
            yield
            two_sided(2, True)
            yield
            for r in range(0, H, CH):
                re, im = product(r)
                re, im = butterfly(*re), butterfly(*im)
                x, y = quads(PH, 0, r), quads(PH, 1, r)
                c, s = quads(CS, 0, r), quads(CS, 1, r)
                xs, ys = [], []
                for i, (h, v) in enumerate(QUADS):
                    W[(1, *place(r, h, v))] = 0.5 * (im[i] * x[i] - re[i] * y[i])
                    xs.append(re[i] * c[i] + im[i] * s[i])
                    ys.append(im[i] * c[i] - re[i] * s[i])
                put(r, butterfly(*xs), butterfly(*ys))
            yield
            two_sided(0, True)
            yield
            for r in range(0, H, CH):
                re, im = product(r)
                re, im = butterfly(*re), butterfly(*im)
                x, y = quads(PS, 0, r), quads(PS, 1, r)
                for i, (h, v) in enumerate(QUADS):
                    W[(0, *place(r, h, v))] = 0.5 * (im[i] * x[i] - re[i] * y[i])
            yield
            for s in range(2):
                for k in range(0, N, CH):
                    g = [pltpu.roll(W[s, k : k + CH, v * H : (v + 1) * H], cr, 1) for v in range(2)]
                    zero = jnp.zeros_like(g[0])
                    here = lane >= cr
                    three = jnp.where(here, g[0], zero), jnp.where(here, g[1], g[0]), jnp.where(here, zero, g[1])
                    for v, x in enumerate(three):
                        at = (s, cq + v, pl.ds(r0 + k, CH), slice(None))
                        O[at] = O[at] + x

        return probe

    chains = chain(0), chain(1)

    def pair(i, _):
        ahead, behind = chains[0](2 * i), chains[1](2 * i + 1)
        next(ahead)
        ends = object()
        while next(behind, ends) is not ends:
            next(ahead, None)
        return 0

    lax.fori_loop(0, probe_count // 2, pair, 0)

    for out, other, first, last in (
        (early_out, True, 3, 5),
        (keep_out, False, 0, 5),
        (late_out, True, 0, 3),
    ):
        for j in range(first, last):
            base = first_row(STEPS[j], other)
            for s in range(2):
                for v in range(4):
                    out[j - first, s, v] = O[s, v, pl.ds(base, H), :]


STEPS = (0, 3, 1, 2, None)
LEVELS = 32766.0


def rows_of(blocks):
    return blocks * H + CH


def encode(blocks, out):
    sublane = lax.broadcasted_iota(jnp.int32, (CH, H), 0)
    logs = jnp.zeros((CH, H), F32)
    for b, block in enumerate(blocks):
        top = jnp.abs(block(0))
        for r in range(CH, H, CH):
            top = jnp.maximum(top, jnp.abs(block(r)))
        top = jnp.max(top, axis=0, keepdims=True)
        log = jnp.ceil(16.0 * jnp.log2(jnp.maximum(top, 1e-30)))
        factor = LEVELS * jnp.exp2(log * (-1.0 / 16.0))
        for r in range(0, H, CH):
            out[b * H + r : b * H + r + CH, :] = jnp.round(block(r) * factor).astype(jnp.int32).astype(jnp.int16)
        logs = jnp.where(sublane == b, log, logs)
    n = len(blocks) * H
    out[n : n + CH, :] = logs.astype(jnp.int32).astype(jnp.int16)


def decoder(code, count):
    n = count * H
    logs = code[n : n + CH, :].astype(jnp.int32).astype(F32)
    scales = jnp.exp2(logs * (1.0 / 16.0)) * (1.0 / LEVELS)

    def rows(b, r, factor=None):
        scale = scales[b : b + 1, :]
        if factor is not None:
            scale = scale * factor
        return code[b * H + r : b * H + r + CH, :].astype(jnp.int32).astype(F32) * scale

    return rows


def here_sum(keep, came, below):
    chip = lax.axis_index("owner") // 2
    both, even, odd = below
    gets = decoder(both, 8), (decoder(even, 4), decoder(odd, 4))

    def cells(j, s, v, r):
        x = keep[j, s, v, r : r + CH, :] + came[j, s, v, r : r + CH, :]
        factor = jnp.where((chip + STEPS[j]) % 4 == 0, 1.0, 0.0)
        return x + gets[0](s * 4 + v, r, factor) + gets[1][s](v, r, factor)

    return cells


def block_of(total, s, v):
    return lambda r: total[s, v, r : r + CH, :]


def below_kernel(keep, came, both, even, odd, total):
    for s in range(2):
        for v in range(4):
            total[s, v] = keep[4, s, v] + came[1, s, v]
    encode([block_of(total, s, v) for s in range(2) for v in range(4)], both)
    for s, out in ((0, even), (1, odd)):
        encode([block_of(total, s, v) for v in range(4)], out)


def relay_kernel(keep, came, out_up, out_down, total):
    for s, out in ((0, out_up), (1, out_down)):
        for v in range(4):
            total[s, v] = keep[3, s, v] + came[0, s, v]
        encode([block_of(total, s, v) for v in range(4)], out)


def sides_kernel(keep, came, *refs):
    cells = here_sum(keep, came, refs[:3])
    from_up, from_down, up, down, total = refs[3:]
    for j, slice_, code, out in ((2, 0, from_up, up), (1, 1, from_down, down)):
        get = decoder(code, 4)
        for s in range(2):
            for v in range(4):
                for r in range(0, H, CH):
                    x = cells(j, s, v, r)
                    total[s, v, r : r + CH, :] = x + get(v, r) if s == slice_ else x
        encode([block_of(total, s, v) for s in range(2) for v in range(4)], out)


def own_kernel(keep, came, *refs):
    cells = here_sum(keep, came, refs[:3])
    gets = [decoder(code, 8) for code in refs[3:5]]
    left, over, total = refs[5:]
    for s in range(2):
        for v in range(4):
            for r in range(0, H, CH):
                x = cells(0, s, v, r)
                for get in gets:
                    x = x + get(s * 4 + v, r)
                if v < 2:
                    left[s, v, r : r + CH, :] = x
                else:
                    total[s, v, r : r + CH, :] = x
    encode([block_of(total, s, v) for s in range(2) for v in (2, 3)], over)


def last_kernel(left, code, out):
    get = decoder(code, 4)
    for s in range(2):
        for v in range(2):
            for r in range(0, H, CH):
                out[s, r : r + CH, v * H : (v + 1) * H] = left[s, v, r : r + CH, :] + get(s * 2 + v, r)


def local(kernel, name, outs, *operands, scratch=True):
    vmem = pl.BlockSpec(memory_space=pltpu.VMEM)
    return pl.pallas_call(
        kernel,
        out_shape=tuple(outs),
        in_specs=[vmem] * len(operands),
        out_specs=(vmem,) * len(outs),
        scratch_shapes=[pltpu.VMEM((2, 4, H, H), F32)] if scratch else [],
        compiler_params=pltpu.CompilerParams(vmem_limit_bytes=16 << 20),
        name=name,
    )(*operands)


def twin(x):
    return lax.ppermute(x, "owner", [(i, i ^ 1) for i in range(lax.axis_size("owner"))])


def hop(x, tile_rows=0, tile_cols=0, chips=0, only=range(4)):
    owners, tiles = lax.axis_size("owner"), lax.axis_size("tile")
    route = []
    for t in range(tiles):
        row, col = t // TX + tile_rows, t % TX + tile_cols
        if 0 <= row < tiles // TX and 0 <= col < TX:
            for o in range(owners):
                if o // 2 in only:
                    route.append((t * owners + o, (row * TX + col) * owners + (o + 2 * chips) % owners))
    return lax.ppermute(x, ("tile", "owner"), route)


def body(potential, positions, illumination, measured):
    own = potential[:, 0]
    layers = own.shape[0]
    chip = lax.axis_index("owner") // 2
    barrier = lax.optimization_barrier
    right = hop(own, tile_cols=-1)
    own_up, own_down = hop(own, chips=1), hop(own, chips=-1)
    right, own_twin = barrier((right, twin(own)))
    right_up, right_down = hop(right, chips=1), hop(right, chips=-1)
    own_far = hop(own_up[:1], chips=1), hop(own_down[1:], chips=-1)
    side_twins = [twin(x) for x in (own_up, own_down, right)]
    right_up, right_down, own_far, side_twins = barrier((right_up, right_down, own_far, side_twins))
    right_far = hop(right_up[:1], chips=1), hop(right_down[1:], chips=-1)
    first = jnp.concatenate(
        [lax.select_n(chip, own, own_up, own, own_down), lax.select_n(chip, right, right_up, right, right_down)],
        axis=2,
    )
    low = (
        hop(first[:1], tile_rows=-1, chips=1, only=(1,)),
        hop(first[1:], tile_rows=-1, chips=-1, only=(3,)),
        hop(first, tile_rows=-1, only=(0, 1, 3)),
    )

    far_twins = [twin(x) for x in (*own_far, right_up, right_down)]
    low, right_far, far_twins = barrier((low, right_far, far_twins))
    low = jnp.where(chip == 2, jnp.concatenate(low[:2]), low[2])

    table = tables()
    fixed = [positions.T, own, illumination, measured]
    fixed += [jnp.asarray(table), jnp.asarray(np.ascontiguousarray(np.swapaxes(table, 2, 3)))]
    fixed += [jnp.asarray(unshuffle())]
    fixed = [pltpu.with_memory_space_constraint(x, pltpu.HBM) for x in fixed]
    vmem = pl.BlockSpec(memory_space=pltpu.VMEM)
    hbm = pl.BlockSpec(memory_space=pltpu.HBM)
    mine = [(0, 0, 0, own), (3, 0, 0, own_up), (1, 0, 0, own_down)]
    mine += [(0, 0, N, right), (3, 0, N, right_up), (1, 0, N, right_down)]
    mine += [(2, 0, 0, own_far[0]), (2, 1, 0, own_far[1])]
    mine += [(2, 0, N, right_far[0]), (2, 1, N, right_far[1])]
    mine.append((None, 0, 0, low))
    pieces = [(k, False, s, c) for k, s, c, _ in mine] + [(k, True, s, c) for k, s, c, _ in mine]
    cells = [x for *_, x in mine[1:]] + [own_twin, *side_twins, *far_twins[2:], *far_twins[:2]]
    cells += [twin(x) for *_, x in mine[8:]]

    field = pltpu.VMEM((2, 2, N, N), F32)
    extended = pltpu.VMEM((layers, 4, 10 * H, H), F32)
    keep, early, late = (jax.ShapeDtypeStruct((n, layers, 4, H, H), F32) for n in (5, 2, 3))

    def kernel(*refs):
        probes_kernel(pieces, *refs)

    keep, early, late = pl.pallas_call(
        kernel,
        out_shape=(keep, early, late),
        in_specs=[hbm] * len(fixed) + [vmem] * len(cells),
        out_specs=(vmem, vmem, vmem),
        scratch_shapes=[
            extended,
            extended,
            field,
            pltpu.VMEM((2, 2, N, 2 * N), BF),
            pltpu.VMEM((2, 2, 2, N, N), BF),
            field,
            field,
            field,
            field,
            pltpu.VMEM((2, 2, H, N), F32),
            pltpu.VMEM((2, 2, N, H), F32),
            pltpu.SMEM((2, 4), jnp.int32),
            *[pltpu.VMEM(x.shape, x.dtype) for x in fixed[1:]],
            pltpu.SemaphoreType.DMA((7,)),
        ],
        compiler_params=pltpu.CompilerParams(vmem_limit_bytes=36 << 20),
        name="probes",
    )(*fixed, *cells)

    whole = jax.ShapeDtypeStruct((rows_of(8), H), jnp.int16)
    half = jax.ShapeDtypeStruct((rows_of(4), H), jnp.int16)
    early = twin(early)
    both, even, odd = local(below_kernel, "below", [whole, half, half], keep, early)
    below = (
        hop(both, tile_rows=1, only=(0, 1, 3)),
        hop(even, tile_rows=1, chips=-1, only=(2,)),
        hop(odd, tile_rows=1, chips=1, only=(2,)),
    )
    from_up, from_down = local(relay_kernel, "relay", [half, half], keep, early)
    came = twin(late)
    from_up, from_down = hop(from_up, chips=1), hop(from_down, chips=-1)
    to_up, to_down = local(sides_kernel, "sides", [whole] * 2, keep, came, *below, from_up, from_down)
    to_up, to_down = hop(to_up, chips=1), hop(to_down, chips=-1)
    left = jax.ShapeDtypeStruct((layers, 2, H, H), F32)
    left, over = local(own_kernel, "own", [left, half], keep, came, *below, to_up, to_down)
    over = hop(over, tile_cols=1)
    result = jax.ShapeDtypeStruct((layers, H, N), F32)
    (result,) = local(last_kernel, "last", [result], left, over, scratch=False)
    return result[:, None]


def solution(mesh):
    in_specs = (
        P(None, "tile", "owner", None),
        P(("tile", "owner"), None),
        P(),
        P(("tile", "owner"), None, None),
    )
    out_specs = P(None, "tile", "owner", None)
    return jax.shard_map(body, mesh=mesh, in_specs=in_specs, out_specs=out_specs, check_vma=False)
```

```python
import numpy as np

import jax
import jax.numpy as jnp
from jax import lax
from jax.experimental import pallas as pl
from jax.experimental.pallas import tpu as pltpu
from jax.sharding import PartitionSpec as P

TX = 8
N = 256
H = 128
CH = 16
BF = jnp.bfloat16
F32 = jnp.float32


def real_block(c):
    return np.block([[c.real, -c.imag], [c.imag, c.real]])


def tables():
    k = np.arange(N)
    signed = (k + H) % N - H
    along = np.exp(-4j * np.pi * signed.astype(np.float64) ** 2 / N**2)
    circulant = np.fft.ifft(along)[(k[:, None] - k[None, :]) % N]
    a, b = circulant[:H, :H], circulant[:H, H:]
    m = np.arange(H)
    even = np.exp(-2j * np.pi * ((2 * m[:, None]) * m[None, :] % N) / N) / 16
    odd = np.exp(-2j * np.pi * ((2 * m[:, None] + 1) * m[None, :] % N) / N) / 16
    full = np.stack([real_block(c) for c in ((a + b) / 2, (a - b) / 2, even, odd)])
    high = full.astype(np.float32).astype(jnp.bfloat16)
    low = (full - high.astype(np.float64)).astype(np.float32).astype(jnp.bfloat16)
    return np.stack([high, low], axis=1)


def unshuffle():
    table = np.zeros((N, N), np.float32)
    for q in range(2):
        for n in range(H):
            table[2 * n + q, q * H + n] = 1
    return table.astype(jnp.bfloat16)


def fitted():
    z = (np.cos(np.pi * (np.arange(400) + 0.5) / 400) + 1) * 18.2
    w = np.sqrt(z)
    out = []
    for values, degree in ((np.cos(w / 2), 7), (np.sin(w / 2) / w, 6)):
        fit = np.polynomial.Chebyshev.fit(z, values, degree, domain=[0, 36.4])
        out.append([float(c) for c in fit.convert(kind=np.polynomial.Polynomial).coef])
    return out


COS, SIN = fitted()


def poly(coefficients, z):
    total = jnp.full_like(z, coefficients[-1])
    for c in coefficients[-2::-1]:
        total = total * z + c
    return total


def cossin(w):
    z = w * w
    return poly(COS, z), w * poly(SIN, z)


def split(x):
    high = x.astype(BF)
    return high, (x - high.astype(F32)).astype(BF)


def butterfly(x00, x01, x10, x11):
    a0, a1 = x00 + x10, x01 + x11
    b0, b1 = x00 - x10, x01 - x11
    return a0 + a1, a0 - a1, b0 + b1, b0 - b1


QUADS = [(h, v) for h in range(2) for v in range(2)]


def probes_kernel(pieces, *refs):
    count = len(pieces)
    sources, parts, refs = refs[:7], list(refs[7 : 6 + count]), refs[6 + count :]
    keep_out, early_out, late_out = refs[:3]
    E, O, *work = refs[3:14]
    positions, here, illum, meas, tab, tabt, perm, sems = refs[14:]
    copies = [
        pltpu.make_async_copy(source, target, sems.at[i])
        for i, (source, target) in enumerate(zip(sources, (positions, here, illum, meas, tab, tabt, perm)))
    ]
    for copy in copies:
        copy.start()
    tile = lax.axis_index("tile")
    owner = lax.axis_index("owner")
    chip, core = owner // 2, owner % 2

    def first_row(step, other):
        chip_rows = 8 if step is None else 2 * ((chip + step) % 4)
        return pl.multiple_of((chip_rows + (1 - core if other else core)) * H, H)

    probe_count = meas.shape[0]
    lane = lax.broadcasted_iota(jnp.int32, (CH, H), 1)

    def clear(i, _):
        r = pl.multiple_of(i * 32, 32)
        for s in range(2):
            for v in range(4):
                O[s, v, pl.ds(r, 32), :] = jnp.zeros((32, H), F32)
        return 0

    lax.fori_loop(0, O.shape[2] // 32, clear, 0)
    copies[1].wait()
    parts.insert(0, here)
    for (step, other, first_slice, first_col), part in zip(pieces, parts):
        base = first_row(step, other)
        slices, height, width = part.shape

        def unpack(i, _, part=part, base=base, slices=slices, width=width, fs=first_slice, fc=first_col):
            r = pl.multiple_of(i * 32, 32)
            for s in range(slices):
                for v in range(width // H):
                    E[fs + s, fc // H + v, pl.ds(base + r, 32), :] = part[
                        s, pl.ds(r, 32), v * H : (v + 1) * H
                    ].astype(F32)
            return 0

        lax.fori_loop(0, height // 32, unpack, 0)
    for i in (0, 2, 3, 4, 5, 6):
        copies[i].wait()
    def chain(slot):
        W, A, B, Z, PS, PH, CS, MP, MS = (ref.at[slot] for ref in work)

        def put(r, re, im):
            for pq in range(4):
                p, q = pq // 2, pq % 2
                for j, x in ((0, re[pq]), (1, im[pq])):
                    high, low = split(x)
                    A[q, pl.ds(p * H + r, CH), j * H : (j + 1) * H] = high
                    A[q, pl.ds(p * H + r, CH), N + j * H : N + (j + 1) * H] = low

        def two_sided(t, adjoint):
            left, right = (tabt, tab) if adjoint else (tab, tabt)
            for q in range(2):
                high, low = right[t + q, 0], right[t + q, 1]
                a = A[q]
                v = jnp.dot(
                    jnp.concatenate([a, a[:, :N]], axis=1),
                    jnp.concatenate([high, high, low], axis=0),
                    preferred_element_type=F32,
                )
                for p in range(2):
                    for j in range(2):
                        x, y = split(v[p * H : (p + 1) * H, j * H : (j + 1) * H])
                        B[p, 0, j * H : (j + 1) * H, q * H : (q + 1) * H] = x
                        B[p, 1, j * H : (j + 1) * H, q * H : (q + 1) * H] = y
            for p in range(2):
                high, low = left[t + p, 0], left[t + p, 1]
                Z[p] = jnp.dot(
                    jnp.concatenate([high, high, low], axis=1),
                    jnp.concatenate([B[p, 0], B[p, 1], B[p, 0]], axis=0),
                    preferred_element_type=F32,
                )

        def product(r):
            re = [Z[p, pl.ds(r, CH), q * H : (q + 1) * H] for p, q in QUADS]
            im = [Z[p, pl.ds(H + r, CH), q * H : (q + 1) * H] for p, q in QUADS]
            return re, im

        def place(r, h, v):
            return slice(h * H + r, h * H + r + CH), slice(v * H, (v + 1) * H)

        def quads(ref, first, r):
            return [ref[(first, *place(r, h, v))] for h, v in QUADS]

        def probe(n):
            r0 = positions[0, n] - tile // TX * (8 * H)
            c0 = positions[1, n] - tile % TX * N
            cq, cr = c0 // H, c0 % H
            back = (H - cr) % H
            for s in range(2):
                for k in range(0, N, CH):
                    y = [pltpu.roll(E[s, cq + v, pl.ds(r0 + k, CH), :], back, 1) for v in range(3)]
                    for v in range(2):
                        W[s, k : k + CH, v * H : (v + 1) * H] = jnp.where(lane < H - cr, y[v], y[v + 1])
            yield
            for v in range(2):
                MS[v] = meas[n, :, v * H : (v + 1) * H]
            for p in range(2):
                m = jnp.concatenate([MS[v, pl.ds(p, H, stride=2), :] for v in range(2)], axis=1)
                MP[p] = jnp.dot(
                    jnp.concatenate(split(m), axis=1),
                    jnp.concatenate([perm[...], perm[...]], axis=0),
                    preferred_element_type=F32,
                )
            yield
            for r in range(0, H, CH):
                w, a, b = quads(W, 0, r), quads(illum, 0, r), quads(illum, 1, r)
                re, im = [], []
                for i, (h, v) in enumerate(QUADS):
                    c, s = cossin(w[i])
                    re.append(a[i] * c - b[i] * s)
                    im.append(a[i] * s + b[i] * c)
                    PS[(0, *place(r, h, v))] = re[i]
                    PS[(1, *place(r, h, v))] = im[i]
                put(r, butterfly(*re), butterfly(*im))
            yield
            two_sided(0, False)
            yield
            for r in range(0, H, CH):
                re, im = product(r)
                re, im = butterfly(*re), butterfly(*im)
                w = quads(W, 1, r)
                xs, ys = [], []
                for i, (h, v) in enumerate(QUADS):
                    c, s = cossin(w[i])
                    xs.append(re[i] * c - im[i] * s)
                    ys.append(re[i] * s + im[i] * c)
                    CS[(0, *place(r, h, v))] = c
                    CS[(1, *place(r, h, v))] = s
                    PH[(0, *place(r, h, v))] = xs[i]
                    PH[(1, *place(r, h, v))] = ys[i]
                put(r, butterfly(*xs), butterfly(*ys))
            yield
            two_sided(2, False)
            yield
            for r in range(0, H, CH):
                re, im = product(r)
                xs, ys = [], []
                for i, (p, q) in enumerate(QUADS):
                    m = MP[p, pl.ds(r, CH), q * H : (q + 1) * H]
                    misfit = 0.5 * (re[i] * re[i] + im[i] * im[i] - m)
                    xs.append(misfit * re[i])
                    ys.append(misfit * im[i])
                put(r, xs, ys)
            yield
            two_sided(2, True)
            yield
            for r in range(0, H, CH):
                re, im = product(r)
                re, im = butterfly(*re), butterfly(*im)
                x, y = quads(PH, 0, r), quads(PH, 1, r)
                c, s = quads(CS, 0, r), quads(CS, 1, r)
                xs, ys = [], []
                for i, (h, v) in enumerate(QUADS):
                    W[(1, *place(r, h, v))] = 0.5 * (im[i] * x[i] - re[i] * y[i])
                    xs.append(re[i] * c[i] + im[i] * s[i])
                    ys.append(im[i] * c[i] - re[i] * s[i])
                put(r, butterfly(*xs), butterfly(*ys))
            yield
            two_sided(0, True)
            yield
            for r in range(0, H, CH):
                re, im = product(r)
                re, im = butterfly(*re), butterfly(*im)
                x, y = quads(PS, 0, r), quads(PS, 1, r)
                for i, (h, v) in enumerate(QUADS):
                    W[(0, *place(r, h, v))] = 0.5 * (im[i] * x[i] - re[i] * y[i])
            yield
            for s in range(2):
                for k in range(0, N, CH):
                    g = [pltpu.roll(W[s, k : k + CH, v * H : (v + 1) * H], cr, 1) for v in range(2)]
                    zero = jnp.zeros_like(g[0])
                    here = lane >= cr
                    three = jnp.where(here, g[0], zero), jnp.where(here, g[1], g[0]), jnp.where(here, zero, g[1])
                    for v, x in enumerate(three):
                        at = (s, cq + v, pl.ds(r0 + k, CH), slice(None))
                        O[at] = O[at] + x

        return probe

    chains = chain(0), chain(1)

    def pair(i, _):
        ahead, behind = chains[0](2 * i), chains[1](2 * i + 1)
        next(ahead)
        ends = object()
        while next(behind, ends) is not ends:
            next(ahead, None)
        return 0

    lax.fori_loop(0, probe_count // 2, pair, 0)

    for out, other, first, last in (
        (early_out, True, 3, 5),
        (keep_out, False, 0, 5),
        (late_out, True, 0, 3),
    ):
        for j in range(first, last):
            base = first_row(STEPS[j], other)
            for s in range(2):
                for v in range(4):
                    out[j - first, s, v] = O[s, v, pl.ds(base, H), :]


STEPS = (0, 3, 1, 2, None)
LEVELS = 32766.0


def rows_of(blocks):
    return blocks * H + CH


def encode(blocks, out):
    sublane = lax.broadcasted_iota(jnp.int32, (CH, H), 0)
    logs = jnp.zeros((CH, H), F32)
    for b, block in enumerate(blocks):
        top = jnp.abs(block(0))
        for r in range(CH, H, CH):
            top = jnp.maximum(top, jnp.abs(block(r)))
        top = jnp.max(top, axis=0, keepdims=True)
        log = jnp.ceil(16.0 * jnp.log2(jnp.maximum(top, 1e-30)))
        factor = LEVELS * jnp.exp2(log * (-1.0 / 16.0))
        for r in range(0, H, CH):
            out[b * H + r : b * H + r + CH, :] = jnp.round(block(r) * factor).astype(jnp.int32).astype(jnp.int16)
        logs = jnp.where(sublane == b, log, logs)
    n = len(blocks) * H
    out[n : n + CH, :] = logs.astype(jnp.int32).astype(jnp.int16)


def decoder(code, count):
    n = count * H
    logs = code[n : n + CH, :].astype(jnp.int32).astype(F32)
    scales = jnp.exp2(logs * (1.0 / 16.0)) * (1.0 / LEVELS)

    def rows(b, r, factor=None):
        scale = scales[b : b + 1, :]
        if factor is not None:
            scale = scale * factor
        return code[b * H + r : b * H + r + CH, :].astype(jnp.int32).astype(F32) * scale

    return rows


def here_sum(keep, came, below):
    chip = lax.axis_index("owner") // 2
    both, even, odd = below
    gets = decoder(both, 8), (decoder(even, 4), decoder(odd, 4))

    def cells(j, s, v, r):
        x = keep[j, s, v, r : r + CH, :] + came[j, s, v, r : r + CH, :]
        factor = jnp.where((chip + STEPS[j]) % 4 == 0, 1.0, 0.0)
        return x + gets[0](s * 4 + v, r, factor) + gets[1][s](v, r, factor)

    return cells


def block_of(total, s, v):
    return lambda r: total[s, v, r : r + CH, :]


def below_kernel(keep, came, both, even, odd, total):
    for s in range(2):
        for v in range(4):
            total[s, v] = keep[4, s, v] + came[1, s, v]
    encode([block_of(total, s, v) for s in range(2) for v in range(4)], both)
    for s, out in ((0, even), (1, odd)):
        encode([block_of(total, s, v) for v in range(4)], out)


def relay_kernel(keep, came, out_up, out_down, total):
    for s, out in ((0, out_up), (1, out_down)):
        for v in range(4):
            total[s, v] = keep[3, s, v] + came[0, s, v]
        encode([block_of(total, s, v) for v in range(4)], out)


def sides_kernel(keep, came, *refs):
    cells = here_sum(keep, came, refs[:3])
    from_up, from_down, up, down, total = refs[3:]
    for j, slice_, code, out in ((2, 0, from_up, up), (1, 1, from_down, down)):
        get = decoder(code, 4)
        for s in range(2):
            for v in range(4):
                for r in range(0, H, CH):
                    x = cells(j, s, v, r)
                    total[s, v, r : r + CH, :] = x + get(v, r) if s == slice_ else x
        encode([block_of(total, s, v) for s in range(2) for v in range(4)], out)


def own_kernel(keep, came, *refs):
    cells = here_sum(keep, came, refs[:3])
    gets = [decoder(code, 8) for code in refs[3:5]]
    left, over, total = refs[5:]
    for s in range(2):
        for v in range(4):
            for r in range(0, H, CH):
                x = cells(0, s, v, r)
                for get in gets:
                    x = x + get(s * 4 + v, r)
                if v < 2:
                    left[s, v, r : r + CH, :] = x
                else:
                    total[s, v, r : r + CH, :] = x
    encode([block_of(total, s, v) for s in range(2) for v in (2, 3)], over)


def last_kernel(left, code, out):
    get = decoder(code, 4)
    for s in range(2):
        for v in range(2):
            for r in range(0, H, CH):
                out[s, r : r + CH, v * H : (v + 1) * H] = left[s, v, r : r + CH, :] + get(s * 2 + v, r)


def local(kernel, name, outs, *operands, scratch=True):
    vmem = pl.BlockSpec(memory_space=pltpu.VMEM)
    return pl.pallas_call(
        kernel,
        out_shape=tuple(outs),
        in_specs=[vmem] * len(operands),
        out_specs=(vmem,) * len(outs),
        scratch_shapes=[pltpu.VMEM((2, 4, H, H), F32)] if scratch else [],
        compiler_params=pltpu.CompilerParams(vmem_limit_bytes=16 << 20),
        name=name,
    )(*operands)


def twin(x):
    return lax.ppermute(x, "owner", [(i, i ^ 1) for i in range(lax.axis_size("owner"))])


def hop(x, tile_rows=0, tile_cols=0, chips=0, only=range(4)):
    owners, tiles = lax.axis_size("owner"), lax.axis_size("tile")
    route = []
    for t in range(tiles):
        row, col = t // TX + tile_rows, t % TX + tile_cols
        if 0 <= row < tiles // TX and 0 <= col < TX:
            for o in range(owners):
                if o // 2 in only:
                    route.append((t * owners + o, (row * TX + col) * owners + (o + 2 * chips) % owners))
    return lax.ppermute(x, ("tile", "owner"), route)


def body(potential, positions, illumination, measured):
    own = potential[:, 0]
    layers = own.shape[0]
    chip = lax.axis_index("owner") // 2
    barrier = lax.optimization_barrier

    def from_below(x):
        return (
            hop(x, tile_rows=-1, only=(0, 1, 3)),
            hop(x[:1], tile_rows=-1, chips=1, only=(1,)),
            hop(x[1:], tile_rows=-1, chips=-1, only=(3,)),
        )

    def joined(x, even, odd):
        return jnp.where(chip == 2, jnp.concatenate([even, odd]), x)

    right = hop(own, tile_cols=-1)
    own_up, own_down = hop(own, chips=1), hop(own, chips=-1)
    right, own_twin = barrier((right, twin(own)))
    right_up, right_down = hop(right, chips=1), hop(right, chips=-1)
    low_own = from_below(lax.select_n(chip, own, own_up, own, own_down))
    own_far = hop(own_up[:1], chips=1), hop(own_down[1:], chips=-1)
    side_twins = [twin(x) for x in (own_up, own_down, right)]
    right_up, right_down, low_own, own_far, side_twins = barrier(
        (right_up, right_down, low_own, own_far, side_twins)
    )
    low_right = from_below(lax.select_n(chip, right, right_up, right, right_down))
    right_far = hop(right_up[:1], chips=1), hop(right_down[1:], chips=-1)
    low_own = joined(*low_own)
    far_twins = [twin(x) for x in (*own_far, right_up, right_down, low_own)]
    low_right, right_far, far_twins = barrier((low_right, right_far, far_twins))
    low_right = joined(*low_right)

    table = tables()
    fixed = [positions.T, own, illumination, measured]
    fixed += [jnp.asarray(table), jnp.asarray(np.ascontiguousarray(np.swapaxes(table, 2, 3)))]
    fixed += [jnp.asarray(unshuffle())]
    fixed = [pltpu.with_memory_space_constraint(x, pltpu.HBM) for x in fixed]
    vmem = pl.BlockSpec(memory_space=pltpu.VMEM)
    hbm = pl.BlockSpec(memory_space=pltpu.HBM)
    mine = [(0, 0, 0, own), (3, 0, 0, own_up), (1, 0, 0, own_down)]
    mine += [(0, 0, N, right), (3, 0, N, right_up), (1, 0, N, right_down)]
    mine += [(2, 0, 0, own_far[0]), (2, 1, 0, own_far[1])]
    mine += [(2, 0, N, right_far[0]), (2, 1, N, right_far[1])]
    mine += [(None, 0, 0, low_own), (None, 0, N, low_right)]
    pieces = [(k, False, s, c) for k, s, c, _ in mine] + [(k, True, s, c) for k, s, c, _ in mine]
    cells = [x for *_, x in mine[1:]] + [own_twin, *side_twins, *far_twins[2:4], *far_twins[:2]]
    cells += [twin(x) for x in right_far] + [far_twins[4], twin(low_right)]

    field = pltpu.VMEM((2, 2, N, N), F32)
    extended = pltpu.VMEM((layers, 4, 10 * H, H), F32)
    keep, early, late = (jax.ShapeDtypeStruct((n, layers, 4, H, H), F32) for n in (5, 2, 3))

    def kernel(*refs):
        probes_kernel(pieces, *refs)

    keep, early, late = pl.pallas_call(
        kernel,
        out_shape=(keep, early, late),
        in_specs=[hbm] * len(fixed) + [vmem] * len(cells),
        out_specs=(vmem, vmem, vmem),
        scratch_shapes=[
            extended,
            extended,
            field,
            pltpu.VMEM((2, 2, N, 2 * N), BF),
            pltpu.VMEM((2, 2, 2, N, N), BF),
            field,
            field,
            field,
            field,
            pltpu.VMEM((2, 2, H, N), F32),
            pltpu.VMEM((2, 2, N, H), F32),
            pltpu.SMEM((2, 4), jnp.int32),
            *[pltpu.VMEM(x.shape, x.dtype) for x in fixed[1:]],
            pltpu.SemaphoreType.DMA((7,)),
        ],
        compiler_params=pltpu.CompilerParams(vmem_limit_bytes=36 << 20),
        name="probes",
    )(*fixed, *cells)

    whole = jax.ShapeDtypeStruct((rows_of(8), H), jnp.int16)
    half = jax.ShapeDtypeStruct((rows_of(4), H), jnp.int16)
    early = twin(early)
    both, even, odd = local(below_kernel, "below", [whole, half, half], keep, early)
    below = (
        hop(both, tile_rows=1, only=(0, 1, 3)),
        hop(even, tile_rows=1, chips=-1, only=(2,)),
        hop(odd, tile_rows=1, chips=1, only=(2,)),
    )
    from_up, from_down = local(relay_kernel, "relay", [half, half], keep, early)
    late, both = barrier((late, both))
    came = twin(late)
    from_up, from_down = hop(from_up, chips=1), hop(from_down, chips=-1)
    to_up, to_down = local(sides_kernel, "sides", [whole] * 2, keep, came, *below, from_up, from_down)
    to_up, to_down = hop(to_up, chips=1), hop(to_down, chips=-1)
    left = jax.ShapeDtypeStruct((layers, 2, H, H), F32)
    left, over = local(own_kernel, "own", [left, half], keep, came, *below, to_up, to_down)
    over = hop(over, tile_cols=1)
    result = jax.ShapeDtypeStruct((layers, H, N), F32)
    (result,) = local(last_kernel, "last", [result], left, over, scratch=False)
    return result[:, None]


def solution(mesh):
    in_specs = (
        P(None, "tile", "owner", None),
        P(("tile", "owner"), None),
        P(),
        P(("tile", "owner"), None, None),
    )
    out_specs = P(None, "tile", "owner", None)
    return jax.shard_map(body, mesh=mesh, in_specs=in_specs, out_specs=out_specs, check_vma=False)
```

```python
import numpy as np

import jax
import jax.numpy as jnp
from jax import lax
from jax.experimental import pallas as pl
from jax.experimental.pallas import tpu as pltpu
from jax.sharding import PartitionSpec as P

TX = 8
N = 256
H = 128
CH = 16
BF = jnp.bfloat16
F32 = jnp.float32


def real_block(c):
    return np.block([[c.real, -c.imag], [c.imag, c.real]])


def tables():
    k = np.arange(N)
    signed = (k + H) % N - H
    along = np.exp(-4j * np.pi * signed.astype(np.float64) ** 2 / N**2)
    circulant = np.fft.ifft(along)[(k[:, None] - k[None, :]) % N]
    a, b = circulant[:H, :H], circulant[:H, H:]
    m = np.arange(H)
    even = np.exp(-2j * np.pi * ((2 * m[:, None]) * m[None, :] % N) / N) / 16
    odd = np.exp(-2j * np.pi * ((2 * m[:, None] + 1) * m[None, :] % N) / N) / 16
    full = np.stack([real_block(c) for c in ((a + b) / 2, (a - b) / 2, even, odd)])
    high = full.astype(np.float32).astype(jnp.bfloat16)
    low = (full - high.astype(np.float64)).astype(np.float32).astype(jnp.bfloat16)
    return np.stack([high, low], axis=1)


def unshuffle():
    table = np.zeros((N, N), np.float32)
    for q in range(2):
        for n in range(H):
            table[2 * n + q, q * H + n] = 1
    return table.astype(jnp.bfloat16)


def fitted():
    z = (np.cos(np.pi * (np.arange(400) + 0.5) / 400) + 1) * 18.2
    w = np.sqrt(z)
    out = []
    for values, degree in ((np.cos(w / 2), 7), (np.sin(w / 2) / w, 6)):
        fit = np.polynomial.Chebyshev.fit(z, values, degree, domain=[0, 36.4])
        out.append([float(c) for c in fit.convert(kind=np.polynomial.Polynomial).coef])
    return out


COS, SIN = fitted()


def poly(coefficients, z):
    total = jnp.full_like(z, coefficients[-1])
    for c in coefficients[-2::-1]:
        total = total * z + c
    return total


def cossin(w):
    z = w * w
    return poly(COS, z), w * poly(SIN, z)


def split(x):
    high = x.astype(BF)
    return high, (x - high.astype(F32)).astype(BF)


def butterfly(x00, x01, x10, x11):
    a0, a1 = x00 + x10, x01 + x11
    b0, b1 = x00 - x10, x01 - x11
    return a0 + a1, a0 - a1, b0 + b1, b0 - b1


QUADS = [(h, v) for h in range(2) for v in range(2)]


def probes_kernel(pieces, *refs):
    count = len(pieces)
    sources, parts, refs = refs[:7], list(refs[7 : 6 + count]), refs[6 + count :]
    keep_out, early_out, late_out = refs[:3]
    E, O, *work = refs[3:14]
    positions, here, illum, meas, tab, tabt, perm, sems = refs[14:]
    copies = [
        pltpu.make_async_copy(source, target, sems.at[i])
        for i, (source, target) in enumerate(zip(sources, (positions, here, illum, meas, tab, tabt, perm)))
    ]
    for copy in copies:
        copy.start()
    tile = lax.axis_index("tile")
    owner = lax.axis_index("owner")
    chip, core = owner // 2, owner % 2

    def first_row(step, other):
        chip_rows = 8 if step is None else 2 * ((chip + step) % 4)
        return pl.multiple_of((chip_rows + (1 - core if other else core)) * H, H)

    probe_count = meas.shape[0]
    lane = lax.broadcasted_iota(jnp.int32, (CH, H), 1)

    def clear(i, _):
        r = pl.multiple_of(i * 32, 32)
        for s in range(2):
            for v in range(4):
                O[s, v, pl.ds(r, 32), :] = jnp.zeros((32, H), F32)
        return 0

    lax.fori_loop(0, O.shape[2] // 32, clear, 0)
    copies[1].wait()
    parts.insert(0, here)
    for (step, other, first_slice, first_col), part in zip(pieces, parts):
        base = first_row(step, other)
        slices, height, width = part.shape

        def unpack(i, _, part=part, base=base, slices=slices, width=width, fs=first_slice, fc=first_col):
            r = pl.multiple_of(i * 32, 32)
            for s in range(slices):
                for v in range(width // H):
                    E[fs + s, fc // H + v, pl.ds(base + r, 32), :] = part[
                        s, pl.ds(r, 32), v * H : (v + 1) * H
                    ].astype(F32)
            return 0

        lax.fori_loop(0, height // 32, unpack, 0)
    for i in (0, 2, 3, 4, 5, 6):
        copies[i].wait()
    def chain(slot):
        W, A, B, Z, PS, PH, CS, MP, MS = (ref.at[slot] for ref in work)

        def put(r, re, im):
            for pq in range(4):
                p, q = pq // 2, pq % 2
                for j, x in ((0, re[pq]), (1, im[pq])):
                    high, low = split(x)
                    A[q, pl.ds(p * H + r, CH), j * H : (j + 1) * H] = high
                    A[q, pl.ds(p * H + r, CH), N + j * H : N + (j + 1) * H] = low

        def two_sided(t, adjoint):
            left, right = (tabt, tab) if adjoint else (tab, tabt)
            for q in range(2):
                high, low = right[t + q, 0], right[t + q, 1]
                a = A[q]
                v = jnp.dot(
                    jnp.concatenate([a, a[:, :N]], axis=1),
                    jnp.concatenate([high, high, low], axis=0),
                    preferred_element_type=F32,
                )
                for p in range(2):
                    for j in range(2):
                        x, y = split(v[p * H : (p + 1) * H, j * H : (j + 1) * H])
                        B[p, 0, j * H : (j + 1) * H, q * H : (q + 1) * H] = x
                        B[p, 1, j * H : (j + 1) * H, q * H : (q + 1) * H] = y
            for p in range(2):
                high, low = left[t + p, 0], left[t + p, 1]
                Z[p] = jnp.dot(
                    jnp.concatenate([high, high, low], axis=1),
                    jnp.concatenate([B[p, 0], B[p, 1], B[p, 0]], axis=0),
                    preferred_element_type=F32,
                )

        def product(r):
            re = [Z[p, pl.ds(r, CH), q * H : (q + 1) * H] for p, q in QUADS]
            im = [Z[p, pl.ds(H + r, CH), q * H : (q + 1) * H] for p, q in QUADS]
            return re, im

        def place(r, h, v):
            return slice(h * H + r, h * H + r + CH), slice(v * H, (v + 1) * H)

        def quads(ref, first, r):
            return [ref[(first, *place(r, h, v))] for h, v in QUADS]

        def probe(n):
            r0 = positions[0, n] - tile // TX * (8 * H)
            c0 = positions[1, n] - tile % TX * N
            cq, cr = c0 // H, c0 % H
            back = (H - cr) % H
            for s in range(2):
                for k in range(0, N, CH):
                    y = [pltpu.roll(E[s, cq + v, pl.ds(r0 + k, CH), :], back, 1) for v in range(3)]
                    for v in range(2):
                        W[s, k : k + CH, v * H : (v + 1) * H] = jnp.where(lane < H - cr, y[v], y[v + 1])
            yield
            for v in range(2):
                MS[v] = meas[n, :, v * H : (v + 1) * H]
            for p in range(2):
                m = jnp.concatenate([MS[v, pl.ds(p, H, stride=2), :] for v in range(2)], axis=1)
                MP[p] = jnp.dot(
                    jnp.concatenate(split(m), axis=1),
                    jnp.concatenate([perm[...], perm[...]], axis=0),
                    preferred_element_type=F32,
                )
            yield
            for r in range(0, H, CH):
                w, a, b = quads(W, 0, r), quads(illum, 0, r), quads(illum, 1, r)
                re, im = [], []
                for i, (h, v) in enumerate(QUADS):
                    c, s = cossin(w[i])
                    re.append(a[i] * c - b[i] * s)
                    im.append(a[i] * s + b[i] * c)
                    PS[(0, *place(r, h, v))] = re[i]
                    PS[(1, *place(r, h, v))] = im[i]
                put(r, butterfly(*re), butterfly(*im))
            yield
            two_sided(0, False)
            yield
            for r in range(0, H, CH):
                re, im = product(r)
                re, im = butterfly(*re), butterfly(*im)
                w = quads(W, 1, r)
                xs, ys = [], []
                for i, (h, v) in enumerate(QUADS):
                    c, s = cossin(w[i])
                    xs.append(re[i] * c - im[i] * s)
                    ys.append(re[i] * s + im[i] * c)
                    CS[(0, *place(r, h, v))] = c
                    CS[(1, *place(r, h, v))] = s
                    PH[(0, *place(r, h, v))] = xs[i]
                    PH[(1, *place(r, h, v))] = ys[i]
                put(r, butterfly(*xs), butterfly(*ys))
            yield
            two_sided(2, False)
            yield
            for r in range(0, H, CH):
                re, im = product(r)
                xs, ys = [], []
                for i, (p, q) in enumerate(QUADS):
                    m = MP[p, pl.ds(r, CH), q * H : (q + 1) * H]
                    misfit = 0.5 * (re[i] * re[i] + im[i] * im[i] - m)
                    xs.append(misfit * re[i])
                    ys.append(misfit * im[i])
                put(r, xs, ys)
            yield
            two_sided(2, True)
            yield
            for r in range(0, H, CH):
                re, im = product(r)
                re, im = butterfly(*re), butterfly(*im)
                x, y = quads(PH, 0, r), quads(PH, 1, r)
                c, s = quads(CS, 0, r), quads(CS, 1, r)
                xs, ys = [], []
                for i, (h, v) in enumerate(QUADS):
                    W[(1, *place(r, h, v))] = 0.5 * (im[i] * x[i] - re[i] * y[i])
                    xs.append(re[i] * c[i] + im[i] * s[i])
                    ys.append(im[i] * c[i] - re[i] * s[i])
                put(r, butterfly(*xs), butterfly(*ys))
            yield
            two_sided(0, True)
            yield
            for r in range(0, H, CH):
                re, im = product(r)
                re, im = butterfly(*re), butterfly(*im)
                x, y = quads(PS, 0, r), quads(PS, 1, r)
                for i, (h, v) in enumerate(QUADS):
                    W[(0, *place(r, h, v))] = 0.5 * (im[i] * x[i] - re[i] * y[i])
            yield
            for s in range(2):
                for k in range(0, N, CH):
                    g = [pltpu.roll(W[s, k : k + CH, v * H : (v + 1) * H], cr, 1) for v in range(2)]
                    zero = jnp.zeros_like(g[0])
                    here = lane >= cr
                    three = jnp.where(here, g[0], zero), jnp.where(here, g[1], g[0]), jnp.where(here, zero, g[1])
                    for v, x in enumerate(three):
                        at = (s, cq + v, pl.ds(r0 + k, CH), slice(None))
                        O[at] = O[at] + x

        return probe

    chains = chain(0), chain(1)

    def pair(i, _):
        ahead, behind = chains[0](2 * i), chains[1](2 * i + 1)
        next(ahead)
        ends = object()
        while next(behind, ends) is not ends:
            next(ahead, None)
        return 0

    lax.fori_loop(0, probe_count // 2, pair, 0)

    for out, first in ((early_out, 3), (late_out, 0)):
        for i in range(out.shape[0]):
            base = first_row(STEPS[first + i], True)

            def block(s, v, base=base):
                return lambda r: O[s, v, pl.ds(pl.multiple_of(base + r, CH), CH), :]

            encode([block(s, v) for s in range(2) for v in range(4)], out.at[i])
    for j, step in enumerate(STEPS):
        base = first_row(step, False)
        for s in range(2):
            for v in range(4):
                keep_out[j, s, v] = O[s, v, pl.ds(base, H), :]


STEPS = (0, 3, 1, 2, None)
LEVELS = 32766.0


def rows_of(blocks):
    return blocks * H + CH


def encode(blocks, out):
    sublane = lax.broadcasted_iota(jnp.int32, (CH, H), 0)
    logs = jnp.zeros((CH, H), F32)
    for b, block in enumerate(blocks):
        top = jnp.abs(block(0))
        for r in range(CH, H, CH):
            top = jnp.maximum(top, jnp.abs(block(r)))
        top = jnp.max(top, axis=0, keepdims=True)
        log = jnp.ceil(16.0 * jnp.log2(jnp.maximum(top, 1e-30)))
        factor = LEVELS * jnp.exp2(log * (-1.0 / 16.0))
        for r in range(0, H, CH):
            out[b * H + r : b * H + r + CH, :] = jnp.round(block(r) * factor).astype(jnp.int32).astype(jnp.int16)
        logs = jnp.where(sublane == b, log, logs)
    n = len(blocks) * H
    out[n : n + CH, :] = logs.astype(jnp.int32).astype(jnp.int16)


def decoder(code, count):
    n = count * H
    logs = code[n : n + CH, :].astype(jnp.int32).astype(F32)
    scales = jnp.exp2(logs * (1.0 / 16.0)) * (1.0 / LEVELS)

    def rows(b, r, factor=None):
        scale = scales[b : b + 1, :]
        if factor is not None:
            scale = scale * factor
        return code[b * H + r : b * H + r + CH, :].astype(jnp.int32).astype(F32) * scale

    return rows


def core_sum(keep, came, j, i):
    get = decoder(came.at[i], 8)
    return lambda s, v, r: keep[j, s, v, r : r + CH, :] + get(s * 4 + v, r)


def here_sum(keep, came, below, j):
    chip = lax.axis_index("owner") // 2
    both, even, odd = below
    gets = decoder(both, 8), (decoder(even, 4), decoder(odd, 4))
    cores = core_sum(keep, came, j, j)
    factor = jnp.where((chip + STEPS[j]) % 4 == 0, 1.0, 0.0)

    def cells(s, v, r):
        return cores(s, v, r) + gets[0](s * 4 + v, r, factor) + gets[1][s](v, r, factor)

    return cells


def block_of(total, s, v):
    return lambda r: total[s, v, r : r + CH, :]


def below_kernel(keep, came, both, even, odd, total):
    cells = core_sum(keep, came, 4, 1)
    for s in range(2):
        for v in range(4):
            for r in range(0, H, CH):
                total[s, v, r : r + CH, :] = cells(s, v, r)
    encode([block_of(total, s, v) for s in range(2) for v in range(4)], both)
    for s, out in ((0, even), (1, odd)):
        encode([block_of(total, s, v) for v in range(4)], out)


def relay_kernel(keep, came, out_up, out_down, total):
    cells = core_sum(keep, came, 3, 0)
    for s, out in ((0, out_up), (1, out_down)):
        for v in range(4):
            for r in range(0, H, CH):
                total[s, v, r : r + CH, :] = cells(s, v, r)
        encode([block_of(total, s, v) for v in range(4)], out)


def sides_kernel(keep, came, *refs):
    from_up, from_down, up, down, total = refs[3:]
    for j, slice_, code, out in ((2, 0, from_up, up), (1, 1, from_down, down)):
        get = decoder(code, 4)
        cells = here_sum(keep, came, refs[:3], j)
        for s in range(2):
            for v in range(4):
                for r in range(0, H, CH):
                    x = cells(s, v, r)
                    total[s, v, r : r + CH, :] = x + get(v, r) if s == slice_ else x
        encode([block_of(total, s, v) for s in range(2) for v in range(4)], out)


def own_kernel(keep, came, *refs):
    cells = here_sum(keep, came, refs[:3], 0)
    gets = [decoder(code, 8) for code in refs[3:5]]
    left, over, total = refs[5:]
    for s in range(2):
        for v in range(4):
            for r in range(0, H, CH):
                x = cells(s, v, r)
                for get in gets:
                    x = x + get(s * 4 + v, r)
                if v < 2:
                    left[s, v, r : r + CH, :] = x
                else:
                    total[s, v, r : r + CH, :] = x
    encode([block_of(total, s, v) for s in range(2) for v in (2, 3)], over)


def last_kernel(left, code, out):
    get = decoder(code, 4)
    for s in range(2):
        for v in range(2):
            for r in range(0, H, CH):
                out[s, r : r + CH, v * H : (v + 1) * H] = left[s, v, r : r + CH, :] + get(s * 2 + v, r)


def local(kernel, name, outs, *operands, scratch=True):
    vmem = pl.BlockSpec(memory_space=pltpu.VMEM)
    return pl.pallas_call(
        kernel,
        out_shape=tuple(outs),
        in_specs=[vmem] * len(operands),
        out_specs=(vmem,) * len(outs),
        scratch_shapes=[pltpu.VMEM((2, 4, H, H), F32)] if scratch else [],
        compiler_params=pltpu.CompilerParams(vmem_limit_bytes=16 << 20),
        name=name,
    )(*operands)


def twin(x):
    return lax.ppermute(x, "owner", [(i, i ^ 1) for i in range(lax.axis_size("owner"))])


def hop(x, tile_rows=0, tile_cols=0, chips=0, only=range(4)):
    owners, tiles = lax.axis_size("owner"), lax.axis_size("tile")
    route = []
    for t in range(tiles):
        row, col = t // TX + tile_rows, t % TX + tile_cols
        if 0 <= row < tiles // TX and 0 <= col < TX:
            for o in range(owners):
                if o // 2 in only:
                    route.append((t * owners + o, (row * TX + col) * owners + (o + 2 * chips) % owners))
    return lax.ppermute(x, ("tile", "owner"), route)


def body(potential, positions, illumination, measured):
    own = potential[:, 0]
    layers = own.shape[0]
    chip = lax.axis_index("owner") // 2
    barrier = lax.optimization_barrier
    right = hop(own, tile_cols=-1)
    own_up, own_down = hop(own, chips=1), hop(own, chips=-1)
    right, own_twin = barrier((right, twin(own)))
    right_up, right_down = hop(right, chips=1), hop(right, chips=-1)
    side_twins = [twin(x) for x in (own_up, own_down, right)]
    right_up, right_down, side_twins = barrier((right_up, right_down, side_twins))
    first = jnp.concatenate(
        [lax.select_n(chip, own, own_up, own, own_down), lax.select_n(chip, right, right_up, right, right_down)],
        axis=2,
    )
    low = (
        hop(first[:1], tile_rows=-1, chips=1, only=(1,)),
        hop(first[1:], tile_rows=-1, chips=-1, only=(3,)),
        hop(first, tile_rows=-1, only=(0, 1, 3)),
    )

    far = (
        hop(jnp.concatenate([own_up[:1], right_up[:1]], axis=2), chips=1),
        hop(jnp.concatenate([own_down[1:], right_down[1:]], axis=2), chips=-1),
    )
    right_twins = [twin(x) for x in (right_up, right_down)]
    low, far, right_twins = barrier((low, far, right_twins))
    low = jnp.where(chip == 2, jnp.concatenate(low[:2]), low[2])

    table = tables()
    fixed = [positions.T, own, illumination, measured]
    fixed += [jnp.asarray(table), jnp.asarray(np.ascontiguousarray(np.swapaxes(table, 2, 3)))]
    fixed += [jnp.asarray(unshuffle())]
    fixed = [pltpu.with_memory_space_constraint(x, pltpu.HBM) for x in fixed]
    vmem = pl.BlockSpec(memory_space=pltpu.VMEM)
    hbm = pl.BlockSpec(memory_space=pltpu.HBM)
    mine = [(0, 0, 0, own), (3, 0, 0, own_up), (1, 0, 0, own_down)]
    mine += [(0, 0, N, right), (3, 0, N, right_up), (1, 0, N, right_down)]
    mine += [(2, 0, 0, far[0]), (2, 1, 0, far[1]), (None, 0, 0, low)]
    pieces = [(k, False, s, c) for k, s, c, _ in mine] + [(k, True, s, c) for k, s, c, _ in mine]
    cells = [x for *_, x in mine[1:]] + [own_twin, *side_twins, *right_twins]
    cells += [twin(x) for *_, x in mine[6:]]

    field = pltpu.VMEM((2, 2, N, N), F32)
    extended = pltpu.VMEM((layers, 4, 10 * H, H), F32)
    keep = jax.ShapeDtypeStruct((5, layers, 4, H, H), F32)
    early, late = (jax.ShapeDtypeStruct((n, rows_of(8), H), jnp.int16) for n in (2, 3))

    def kernel(*refs):
        probes_kernel(pieces, *refs)

    keep, early, late = pl.pallas_call(
        kernel,
        out_shape=(keep, early, late),
        in_specs=[hbm] * len(fixed) + [vmem] * len(cells),
        out_specs=(vmem, vmem, vmem),
        scratch_shapes=[
            extended,
            extended,
            field,
            pltpu.VMEM((2, 2, N, 2 * N), BF),
            pltpu.VMEM((2, 2, 2, N, N), BF),
            field,
            field,
            field,
            field,
            pltpu.VMEM((2, 2, H, N), F32),
            pltpu.VMEM((2, 2, N, H), F32),
            pltpu.SMEM((2, 4), jnp.int32),
            *[pltpu.VMEM(x.shape, x.dtype) for x in fixed[1:]],
            pltpu.SemaphoreType.DMA((7,)),
        ],
        compiler_params=pltpu.CompilerParams(vmem_limit_bytes=36 << 20),
        name="probes",
    )(*fixed, *cells)

    whole = jax.ShapeDtypeStruct((rows_of(8), H), jnp.int16)
    half = jax.ShapeDtypeStruct((rows_of(4), H), jnp.int16)
    early = twin(early)
    both, even, odd = local(below_kernel, "below", [whole, half, half], keep, early)
    below = (
        hop(both, tile_rows=1, only=(0, 1, 3)),
        hop(even, tile_rows=1, chips=-1, only=(2,)),
        hop(odd, tile_rows=1, chips=1, only=(2,)),
    )
    from_up, from_down = local(relay_kernel, "relay", [half, half], keep, early)
    came = twin(late)
    from_up, from_down = hop(from_up, chips=1), hop(from_down, chips=-1)
    to_up, to_down = local(sides_kernel, "sides", [whole] * 2, keep, came, *below, from_up, from_down)
    to_up, to_down = hop(to_up, chips=1), hop(to_down, chips=-1)
    left = jax.ShapeDtypeStruct((layers, 2, H, H), F32)
    left, over = local(own_kernel, "own", [left, half], keep, came, *below, to_up, to_down)
    over = hop(over, tile_cols=1)
    result = jax.ShapeDtypeStruct((layers, H, N), F32)
    (result,) = local(last_kernel, "last", [result], left, over, scratch=False)
    return result[:, None]


def solution(mesh):
    in_specs = (
        P(None, "tile", "owner", None),
        P(("tile", "owner"), None),
        P(),
        P(("tile", "owner"), None, None),
    )
    out_specs = P(None, "tile", "owner", None)
    return jax.shard_map(body, mesh=mesh, in_specs=in_specs, out_specs=out_specs, check_vma=False)
```

```python
import numpy as np

import jax
import jax.numpy as jnp
from jax import lax
from jax.experimental import pallas as pl
from jax.experimental.pallas import tpu as pltpu
from jax.sharding import PartitionSpec as P


TX = 8
N = 256
H = 128
CH = 16
BF = jnp.bfloat16
F32 = jnp.float32


def real_block(c):
    return np.block([[c.real, -c.imag], [c.imag, c.real]])


def tables():
    k = np.arange(N)
    signed = (k + H) % N - H
    along = np.exp(-4j * np.pi * signed.astype(np.float64) ** 2 / N**2)
    circulant = np.fft.ifft(along)[(k[:, None] - k[None, :]) % N]
    a, b = circulant[:H, :H], circulant[:H, H:]
    m = np.arange(H)
    even = np.exp(-2j * np.pi * ((2 * m[:, None]) * m[None, :] % N) / N) / 16
    odd = np.exp(-2j * np.pi * ((2 * m[:, None] + 1) * m[None, :] % N) / N) / 16
    full = np.stack([real_block(c) for c in ((a + b) / 2, (a - b) / 2, even, odd)])
    high = full.astype(np.float32).astype(jnp.bfloat16)
    low = (full - high.astype(np.float64)).astype(np.float32).astype(jnp.bfloat16)
    return np.stack([high, low], axis=1)


def unshuffle():
    table = np.zeros((N, N), np.float32)
    for q in range(2):
        for n in range(H):
            table[2 * n + q, q * H + n] = 1
    return table.astype(jnp.bfloat16)


def fitted():
    z = (np.cos(np.pi * (np.arange(400) + 0.5) / 400) + 1) * 18.2
    w = np.sqrt(z)
    out = []
    for values, degree in ((np.cos(w / 2), 7), (np.sin(w / 2) / w, 6)):
        fit = np.polynomial.Chebyshev.fit(z, values, degree, domain=[0, 36.4])
        out.append([float(c) for c in fit.convert(kind=np.polynomial.Polynomial).coef])
    return out


COS, SIN = fitted()


def poly(coefficients, z):
    total = jnp.full_like(z, coefficients[-1])
    for c in coefficients[-2::-1]:
        total = total * z + c
    return total


def cossin(w):
    z = w * w
    return poly(COS, z), w * poly(SIN, z)


def split(x):
    high = x.astype(BF)
    return high, (x - high.astype(F32)).astype(BF)


def butterfly(x00, x01, x10, x11):
    a0, a1 = x00 + x10, x01 + x11
    b0, b1 = x00 - x10, x01 - x11
    return a0 + a1, a0 - a1, b0 + b1, b0 - b1


QUADS = [(h, v) for h in range(2) for v in range(2)]


def probes_kernel(pieces, *refs):
    count = len(pieces)
    sources, parts, refs = refs[:7], list(refs[7 : 6 + count]), refs[6 + count :]
    keep_out, early_out, late_out = refs[:3]
    E, O, *work = refs[3:14]
    positions, here, illum, meas, tab, tabt, perm, sems = refs[14:]
    copies = [
        pltpu.make_async_copy(source, target, sems.at[i])
        for i, (source, target) in enumerate(zip(sources, (positions, here, illum, meas, tab, tabt, perm)))
    ]
    for copy in copies:
        copy.start()
    tile = lax.axis_index("tile")
    owner = lax.axis_index("owner")
    chip, core = owner // 2, owner % 2

    def first_row(step, other):
        chip_rows = 8 if step is None else 2 * ((chip + step) % 4)
        return pl.multiple_of((chip_rows + (1 - core if other else core)) * H, H)

    probe_count = meas.shape[0]
    lane = lax.broadcasted_iota(jnp.int32, (CH, H), 1)

    def clear(i, _):
        r = pl.multiple_of(i * 32, 32)
        for s in range(2):
            for v in range(4):
                O[s, v, pl.ds(r, 32), :] = jnp.zeros((32, H), F32)
        return 0

    lax.fori_loop(0, O.shape[2] // 32, clear, 0)
    copies[1].wait()
    parts.insert(0, here)
    for (step, other, first_slice, first_col), part in zip(pieces, parts):
        base = first_row(step, other)
        slices, height, width = part.shape

        def unpack(i, _, part=part, base=base, slices=slices, width=width, fs=first_slice, fc=first_col):
            r = pl.multiple_of(i * 32, 32)
            for s in range(slices):
                for v in range(width // H):
                    E[fs + s, fc // H + v, pl.ds(base + r, 32), :] = part[
                        s, pl.ds(r, 32), v * H : (v + 1) * H
                    ].astype(F32)
            return 0

        lax.fori_loop(0, height // 32, unpack, 0)
    for i in (0, 2, 3, 4, 5, 6):
        copies[i].wait()

    def chain(slot):
        W, A, B, Z, PS, PH, CS, MP, MS = (ref.at[slot] for ref in work)

        def put(r, re, im):
            for pq in range(4):
                p, q = pq // 2, pq % 2
                for j, x in ((0, re[pq]), (1, im[pq])):
                    high, low = split(x)
                    A[q, pl.ds(p * H + r, CH), j * H : (j + 1) * H] = high
                    A[q, pl.ds(p * H + r, CH), N + j * H : N + (j + 1) * H] = low

        def two_sided(t, adjoint):
            left, right = (tabt, tab) if adjoint else (tab, tabt)
            for q in range(2):
                high, low = right[t + q, 0], right[t + q, 1]
                a = A[q]
                v = jnp.dot(
                    jnp.concatenate([a, a[:, :N]], axis=1),
                    jnp.concatenate([high, high, low], axis=0),
                    preferred_element_type=F32,
                )
                for p in range(2):
                    for j in range(2):
                        x, y = split(v[p * H : (p + 1) * H, j * H : (j + 1) * H])
                        B[p, 0, j * H : (j + 1) * H, q * H : (q + 1) * H] = x
                        B[p, 1, j * H : (j + 1) * H, q * H : (q + 1) * H] = y
            for p in range(2):
                high, low = left[t + p, 0], left[t + p, 1]
                Z[p] = jnp.dot(
                    jnp.concatenate([high, high, low], axis=1),
                    jnp.concatenate([B[p, 0], B[p, 1], B[p, 0]], axis=0),
                    preferred_element_type=F32,
                )

        def product(r):
            re = [Z[p, pl.ds(r, CH), q * H : (q + 1) * H] for p, q in QUADS]
            im = [Z[p, pl.ds(H + r, CH), q * H : (q + 1) * H] for p, q in QUADS]
            return re, im

        def place(r, h, v):
            return slice(h * H + r, h * H + r + CH), slice(v * H, (v + 1) * H)

        def quads(ref, first, r):
            return [ref[(first, *place(r, h, v))] for h, v in QUADS]

        def probe(n):
            r0 = positions[0, n] - tile // TX * (8 * H)
            c0 = positions[1, n] - tile % TX * N
            cq, cr = c0 // H, c0 % H
            back = (H - cr) % H
            for s in range(2):
                for k in range(0, N, CH):
                    y = [pltpu.roll(E[s, cq + v, pl.ds(r0 + k, CH), :], back, 1) for v in range(3)]
                    for v in range(2):
                        W[s, k : k + CH, v * H : (v + 1) * H] = jnp.where(lane < H - cr, y[v], y[v + 1])
            yield
            for v in range(2):
                MS[v] = meas[n, :, v * H : (v + 1) * H]
            for p in range(2):
                m = jnp.concatenate([MS[v, pl.ds(p, H, stride=2), :] for v in range(2)], axis=1)
                MP[p] = jnp.dot(
                    jnp.concatenate(split(m), axis=1),
                    jnp.concatenate([perm[...], perm[...]], axis=0),
                    preferred_element_type=F32,
                )
            yield
            for r in range(0, H, CH):
                w, a, b = quads(W, 0, r), quads(illum, 0, r), quads(illum, 1, r)
                re, im = [], []
                for i, (h, v) in enumerate(QUADS):
                    c, s = cossin(w[i])
                    re.append(a[i] * c - b[i] * s)
                    im.append(a[i] * s + b[i] * c)
                    PS[(0, *place(r, h, v))] = re[i]
                    PS[(1, *place(r, h, v))] = im[i]
                put(r, butterfly(*re), butterfly(*im))
            yield
            two_sided(0, False)
            yield
            for r in range(0, H, CH):
                re, im = product(r)
                re, im = butterfly(*re), butterfly(*im)
                w = quads(W, 1, r)
                xs, ys = [], []
                for i, (h, v) in enumerate(QUADS):
                    c, s = cossin(w[i])
                    xs.append(re[i] * c - im[i] * s)
                    ys.append(re[i] * s + im[i] * c)
                    CS[(0, *place(r, h, v))] = c
                    CS[(1, *place(r, h, v))] = s
                    PH[(0, *place(r, h, v))] = xs[i]
                    PH[(1, *place(r, h, v))] = ys[i]
                put(r, butterfly(*xs), butterfly(*ys))
            yield
            two_sided(2, False)
            yield
            for r in range(0, H, CH):
                re, im = product(r)
                xs, ys = [], []
                for i, (p, q) in enumerate(QUADS):
                    m = MP[p, pl.ds(r, CH), q * H : (q + 1) * H]
                    misfit = 0.5 * (re[i] * re[i] + im[i] * im[i] - m)
                    xs.append(misfit * re[i])
                    ys.append(misfit * im[i])
                put(r, xs, ys)
            yield
            two_sided(2, True)
            yield
            for r in range(0, H, CH):
                re, im = product(r)
                re, im = butterfly(*re), butterfly(*im)
                x, y = quads(PH, 0, r), quads(PH, 1, r)
                c, s = quads(CS, 0, r), quads(CS, 1, r)
                xs, ys = [], []
                for i, (h, v) in enumerate(QUADS):
                    W[(1, *place(r, h, v))] = 0.5 * (im[i] * x[i] - re[i] * y[i])
                    xs.append(re[i] * c[i] + im[i] * s[i])
                    ys.append(im[i] * c[i] - re[i] * s[i])
                put(r, butterfly(*xs), butterfly(*ys))
            yield
            two_sided(0, True)
            yield
            for r in range(0, H, CH):
                re, im = product(r)
                re, im = butterfly(*re), butterfly(*im)
                x, y = quads(PS, 0, r), quads(PS, 1, r)
                for i, (h, v) in enumerate(QUADS):
                    W[(0, *place(r, h, v))] = 0.5 * (im[i] * x[i] - re[i] * y[i])
            yield
            for s in range(2):
                for k in range(0, N, CH):
                    g = [pltpu.roll(W[s, k : k + CH, v * H : (v + 1) * H], cr, 1) for v in range(2)]
                    zero = jnp.zeros_like(g[0])
                    here = lane >= cr
                    three = jnp.where(here, g[0], zero), jnp.where(here, g[1], g[0]), jnp.where(here, zero, g[1])
                    for v, x in enumerate(three):
                        at = (s, cq + v, pl.ds(r0 + k, CH), slice(None))
                        O[at] = O[at] + x

        return probe

    chains = chain(0), chain(1)

    def pair(i, _):
        ahead, behind = chains[0](2 * i), chains[1](2 * i + 1)
        next(ahead)
        ends = object()
        while next(behind, ends) is not ends:
            next(ahead, None)
        return 0

    lax.fori_loop(0, probe_count // 2, pair, 0)

    for out, first in ((early_out, 3), (late_out, 0)):
        for i in range(out.shape[0]):
            base = first_row(STEPS[first + i], True)

            def block(s, v, base=base):
                return lambda r: O[s, v, pl.ds(pl.multiple_of(base + r, CH), CH), :]

            encode([block(s, v) for s in range(2) for v in range(4)], out.at[i])
    for j, step in enumerate(STEPS):
        base = first_row(step, False)
        for s in range(2):
            for v in range(4):
                keep_out[j, s, v] = O[s, v, pl.ds(base, H), :]


STEPS = (0, 3, 1, 2, None)
LEVELS = 32766.0


def rows_of(blocks):
    return blocks * H + CH


def encode(blocks, out):
    sublane = lax.broadcasted_iota(jnp.int32, (CH, H), 0)
    logs = jnp.zeros((CH, H), F32)
    for b, block in enumerate(blocks):
        top = jnp.abs(block(0))
        for r in range(CH, H, CH):
            top = jnp.maximum(top, jnp.abs(block(r)))
        top = jnp.max(top, axis=0, keepdims=True)
        log = jnp.ceil(16.0 * jnp.log2(jnp.maximum(top, 1e-30)))
        factor = LEVELS * jnp.exp2(log * (-1.0 / 16.0))
        for r in range(0, H, CH):
            out[b * H + r : b * H + r + CH, :] = jnp.round(block(r) * factor).astype(jnp.int32).astype(jnp.int16)
        logs = jnp.where(sublane == b, log, logs)
    n = len(blocks) * H
    out[n : n + CH, :] = logs.astype(jnp.int32).astype(jnp.int16)


def decoder(code, count):
    n = count * H
    logs = code[n : n + CH, :].astype(jnp.int32).astype(F32)
    scales = jnp.exp2(logs * (1.0 / 16.0)) * (1.0 / LEVELS)

    def rows(b, r, factor=None):
        scale = scales[b : b + 1, :]
        if factor is not None:
            scale = scale * factor
        return code[b * H + r : b * H + r + CH, :].astype(jnp.int32).astype(F32) * scale

    return rows


def core_sum(keep, came, j, i):
    get = decoder(came.at[i], 8)
    return lambda s, v, r: keep[j, s, v, r : r + CH, :] + get(s * 4 + v, r)


def here_sum(keep, came, below, j):
    chip = lax.axis_index("owner") // 2
    both, even, odd = below
    gets = decoder(both, 8), (decoder(even, 4), decoder(odd, 4))
    cores = core_sum(keep, came, j, j)
    factor = jnp.where((chip + STEPS[j]) % 4 == 0, 1.0, 0.0)

    def cells(s, v, r):
        return cores(s, v, r) + gets[0](s * 4 + v, r, factor) + gets[1][s](v, r, factor)

    return cells


def block_of(total, s, v):
    return lambda r: total[s, v, r : r + CH, :]


def below_kernel(keep, came, both, total):
    cells = core_sum(keep, came, 4, 1)
    for s in range(2):
        for v in range(4):
            for r in range(0, H, CH):
                total[s, v, r : r + CH, :] = cells(s, v, r)
    encode([block_of(total, s, v) for s in range(2) for v in range(4)], both)


def relay_kernel(keep, came, out_up, out_down, even, odd, total):
    for j, i, outs in ((3, 0, (out_up, out_down)), (4, 1, (even, odd))):
        cells = core_sum(keep, came, j, i)
        for s, out in enumerate(outs):
            for v in range(4):
                for r in range(0, H, CH):
                    total[s, v, r : r + CH, :] = cells(s, v, r)
            encode([block_of(total, s, v) for v in range(4)], out)


def sides_kernel(keep, came, *refs):
    from_up, from_down, *below, up, down, total = refs
    for j, slice_, code, out in ((2, 0, from_up, up), (1, 1, from_down, down)):
        get = decoder(code, 4)
        cells = here_sum(keep, came, below, j)
        for s in range(2):
            for v in range(4):
                for r in range(0, H, CH):
                    x = cells(s, v, r)
                    total[s, v, r : r + CH, :] = x + get(v, r) if s == slice_ else x
        encode([block_of(total, s, v) for s in range(2) for v in range(4)], out)


def own_kernel(keep, came, *refs):
    cells = here_sum(keep, came, refs[:3], 0)
    gets = [decoder(code, 8) for code in refs[3:5]]
    left, over, total = refs[5:]
    for s in range(2):
        for v in range(4):
            for r in range(0, H, CH):
                x = cells(s, v, r)
                for get in gets:
                    x = x + get(s * 4 + v, r)
                if v < 2:
                    left[s, v, r : r + CH, :] = x
                else:
                    total[s, v, r : r + CH, :] = x
    encode([block_of(total, s, v) for s in range(2) for v in (2, 3)], over)


def last_kernel(left, code, out):
    get = decoder(code, 4)
    for s in range(2):
        for v in range(2):
            for r in range(0, H, CH):
                out[s, r : r + CH, v * H : (v + 1) * H] = left[s, v, r : r + CH, :] + get(s * 2 + v, r)


def local(kernel, outs, *operands, scratch=True):
    vmem = pl.BlockSpec(memory_space=pltpu.VMEM)
    return pl.pallas_call(
        kernel,
        out_shape=tuple(outs),
        in_specs=[vmem] * len(operands),
        out_specs=(vmem,) * len(outs),
        scratch_shapes=[pltpu.VMEM((2, 4, H, H), F32)] if scratch else [],
        compiler_params=pltpu.CompilerParams(vmem_limit_bytes=16 << 20),
    )(*operands)


def twin(x):
    return lax.ppermute(x, "owner", [(i, i ^ 1) for i in range(lax.axis_size("owner"))])


def hop(x, tile_rows=0, tile_cols=0, chips=0, only=range(4)):
    owners, tiles = lax.axis_size("owner"), lax.axis_size("tile")
    route = []
    for t in range(tiles):
        row, col = t // TX + tile_rows, t % TX + tile_cols
        if 0 <= row < tiles // TX and 0 <= col < TX:
            for o in range(owners):
                if o // 2 in only:
                    route.append((t * owners + o, (row * TX + col) * owners + (o + 2 * chips) % owners))
    return lax.ppermute(x, ("tile", "owner"), route)


def body(potential, positions, illumination, measured):
    own = potential[:, 0]
    layers = own.shape[0]
    chip = lax.axis_index("owner") // 2
    barrier = lax.optimization_barrier
    right = hop(own, tile_cols=-1)
    own_up, own_down = hop(own, chips=1), hop(own, chips=-1)
    right, own_twin = barrier((right, twin(own)))
    right_up, right_down = hop(right, chips=1), hop(right, chips=-1)
    side_twins = [twin(x) for x in (own_up, own_down, right)]
    right_up, right_down, side_twins = barrier((right_up, right_down, side_twins))
    first = jnp.concatenate(
        [lax.select_n(chip, own, own_up, own, own_down), lax.select_n(chip, right, right_up, right, right_down)],
        axis=2,
    )
    low = (
        hop(first[:1], tile_rows=-1, chips=1, only=(1,)),
        hop(first[1:], tile_rows=-1, chips=-1, only=(3,)),
        hop(first, tile_rows=-1, only=(0, 1, 3)),
    )

    far = (
        hop(jnp.concatenate([own_up[:1], right_up[:1]], axis=2), chips=1),
        hop(jnp.concatenate([own_down[1:], right_down[1:]], axis=2), chips=-1),
    )
    right_twins = [twin(x) for x in (right_up, right_down)]
    low, far, right_twins = barrier((low, far, right_twins))
    low = jnp.where(chip == 2, jnp.concatenate(low[:2]), low[2])

    table = tables()
    fixed = [positions.T, own, illumination, measured]
    fixed += [jnp.asarray(table), jnp.asarray(np.ascontiguousarray(np.swapaxes(table, 2, 3)))]
    fixed += [jnp.asarray(unshuffle())]
    fixed = [pltpu.with_memory_space_constraint(x, pltpu.HBM) for x in fixed]
    vmem = pl.BlockSpec(memory_space=pltpu.VMEM)
    hbm = pl.BlockSpec(memory_space=pltpu.HBM)
    mine = [(0, 0, 0, own), (3, 0, 0, own_up), (1, 0, 0, own_down)]
    mine += [(0, 0, N, right), (3, 0, N, right_up), (1, 0, N, right_down)]
    mine += [(2, 0, 0, far[0]), (2, 1, 0, far[1]), (None, 0, 0, low)]
    pieces = [(k, False, s, c) for k, s, c, _ in mine] + [(k, True, s, c) for k, s, c, _ in mine]
    cells = [x for *_, x in mine[1:]] + [own_twin, *side_twins, *right_twins]
    cells += [twin(x) for *_, x in mine[6:]]

    field = pltpu.VMEM((2, 2, N, N), F32)
    extended = pltpu.VMEM((layers, 4, 10 * H, H), F32)
    keep = jax.ShapeDtypeStruct((5, layers, 4, H, H), F32)
    early, late = (jax.ShapeDtypeStruct((n, rows_of(8), H), jnp.int16) for n in (2, 3))

    def kernel(*refs):
        probes_kernel(pieces, *refs)

    keep, early, late = pl.pallas_call(
        kernel,
        out_shape=(keep, early, late),
        in_specs=[hbm] * len(fixed) + [vmem] * len(cells),
        out_specs=(vmem, vmem, vmem),
        scratch_shapes=[
            extended,
            extended,
            field,
            pltpu.VMEM((2, 2, N, 2 * N), BF),
            pltpu.VMEM((2, 2, 2, N, N), BF),
            field,
            field,
            field,
            field,
            pltpu.VMEM((2, 2, H, N), F32),
            pltpu.VMEM((2, 2, N, H), F32),
            pltpu.SMEM((2, 4), jnp.int32),
            *[pltpu.VMEM(x.shape, x.dtype) for x in fixed[1:]],
            pltpu.SemaphoreType.DMA((7,)),
        ],
        compiler_params=pltpu.CompilerParams(vmem_limit_bytes=36 << 20),
        name="probes",
    )(*fixed, *cells)

    whole = jax.ShapeDtypeStruct((rows_of(8), H), jnp.int16)
    half = jax.ShapeDtypeStruct((rows_of(4), H), jnp.int16)
    early = twin(early)
    (both,) = local(below_kernel, [whole], keep, early)
    from_up, from_down, even, odd = local(relay_kernel, [half] * 4, keep, early)
    came = twin(late)
    both = hop(both, tile_rows=1, only=(0, 1, 3))
    from_up = hop(from_up, chips=1)
    from_down = hop(from_down, chips=-1)
    even = hop(even, tile_rows=1, chips=-1, only=(2,))
    odd = hop(odd, tile_rows=1, chips=1, only=(2,))
    below = both, even, odd
    to_up, to_down = local(sides_kernel, [whole] * 2, keep, came, from_up, from_down, *below)
    to_up, to_down = hop(to_up, chips=1), hop(to_down, chips=-1)
    left = jax.ShapeDtypeStruct((layers, 2, H, H), F32)
    left, over = local(own_kernel, [left, half], keep, came, *below, to_up, to_down)
    over = hop(over, tile_cols=1)
    result = jax.ShapeDtypeStruct((layers, H, N), F32)
    (result,) = local(last_kernel, [result], left, over, scratch=False)
    return result[:, None]


def solution(mesh):
    in_specs = (
        P(None, "tile", "owner", None),
        P(("tile", "owner"), None),
        P(),
        P(("tile", "owner"), None, None),
    )
    out_specs = P(None, "tile", "owner", None)
    return jax.shard_map(body, mesh=mesh, in_specs=in_specs, out_specs=out_specs, check_vma=False)
```
